32 devices in a mesh: fsdp: 8 (over z, x), head: 2 (over core), tensor: 2 (over y).
Axes of the slice: x: 2, y: 2, z: 4, core: 2. Of those that a mesh axis runs over, the one named last changes fastest.
Arguments:
- block_in: bfloat16 [4096, 1024], P('fsdp'), may hold values from -6 to 6
- cotangent: bfloat16 [4096, 1024], P('fsdp'), may hold values from -6 to 6
- norm_gain: float32 [1024], replicated, may hold values from 0.5 to 1.5
- w_x: bfloat16 [1024, 32, 64], P('fsdp', 'head', 'tensor'), may hold values from -0.1875 to 0.1875
- w_z: bfloat16 [1024, 32, 64], P('fsdp', 'head', 'tensor'), may hold values from -0.1875 to 0.1875
- w_bc: bfloat16 [1024, 2, 128], P('fsdp'), may hold values from -0.1875 to 0.1875
- w_dt: bfloat16 [1024, 32], P('fsdp', 'head'), may hold values from -0.1875 to 0.1875
- conv_x: float32 [32, 64, 4], P('head', 'tensor'), may hold values from -3 to 3
- conv_bc: float32 [2, 128, 4], replicated, may hold values from -3 to 3
- dt_bias: float32 [32], P('head'), may hold values from -6 to -2
- a_log: float32 [32], P('head'), may hold values from -1.5 to 0.5
- skip: float32 [32], P('head'), may hold values from 0.5 to 1.5
- gate_gain: float32 [32, 64], P('head', 'tensor'), may hold values from 0.5 to 1.5
- w_out: bfloat16 [32, 64, 1024], P('head', 'tensor', 'fsdp'), may hold values from -0.125 to 0.125
Outputs:
- block_out: bfloat16 [4096, 1024], P('fsdp')
- grad_in: float32 [4096, 1024], P('fsdp')
- grad_norm_gain: float32 [1024], replicated
- grad_w_x: float32 [1024, 32, 64], P('fsdp', 'head', 'tensor')
- grad_w_z: float32 [1024, 32, 64], P('fsdp', 'head', 'tensor')
- grad_w_bc: float32 [1024, 2, 128], P('fsdp')
- grad_w_dt: float32 [1024, 32], P('fsdp', 'head')
- grad_conv_x: float32 [32, 64, 4], P('head', 'tensor')
- grad_conv_bc: float32 [2, 128, 4], replicated
- grad_dt_bias: float32 [32], P('head')
- grad_a_log: float32 [32], P('head')
- grad_skip: float32 [32], P('head')
- grad_gate_gain: float32 [32, 64], P('head', 'tensor')
- grad_w_out: float32 [32, 64, 1024], P('head', 'tensor', 'fsdp')
The draws below stay inside these ranges and needn't reach their ends.
All inputs are finite; a program needn't handle non-finite values.
Results may differ from the reference program's by a relative error of at most 0.011.
Values may be sent and summed in bfloat16 or wider, within the bound.
A program may use at most 128 MiB of HBM per device.

```python
from functools import partial
import jax
import jax.numpy as jnp
from jax import lax

D = 1024
NH = 32
HD = 64
N = 128
K = 4
SPAN = 256
LEN = 512
DI = 2048
SEQS = 8
TOKENS = 4096


def raised(entries, stream_key, source, target, shards_of, factor):
    owner, partner = [(jnp.arange(entries.shape[axis_at]) // (entries.shape[axis_at] // shards_of)).reshape([-1 if axis == axis_at else 1 for axis in range(entries.ndim)]) for axis_at in (source, target)]
    chosen = jax.random.permutation(stream_key, shards_of)[partner]
    strong = (owner == chosen) | (owner == (partner + shards_of // 2) % shards_of)
    return jnp.where(strong, factor * entries, entries)


def level_of(stream_key, dims, pieces, low, top_value):
    gain = 1.0
    for axis_at, blocks in pieces:
        steps = jax.random.uniform(jax.random.fold_in(jax.random.fold_in(stream_key, 6), axis_at), (blocks,), jnp.float32, low / len(pieces), top_value / len(pieces))
        gain = gain * jnp.repeat(jnp.exp(steps), dims[axis_at] // blocks).reshape((-1,) + (1,) * (len(dims) - 1 - axis_at))
    return gain


def scatter_about(key, shape, scale, reach, pieces=(), dtype=jnp.bfloat16):
    drawn = jax.random.normal(key, shape, jnp.float32) * scale
    if len(pieces) > 0:
        drawn = level_of(key, shape, pieces, -0.22, 0.18) * drawn
    return jnp.clip(drawn, min=-reach, max=reach).astype(dtype)


def bell_draw_with(own_key, shape, width, limit, pieces, heavy, kind=jnp.bfloat16):
    entries = width * jax.random.normal(own_key, shape, jnp.float32)
    if pieces:
        entries = entries * level_of(own_key, shape, pieces, -0.22, 0.18)
    return jnp.clip(raised(entries, jax.random.fold_in(own_key, 3), *heavy), -limit, limit).astype(kind)


def setup_inputs(seed: int = 0) -> dict:
    key_of = jax.random.split(jax.random.key(seed), 15)
    block_in = bell_draw_with(key_of[0], (TOKENS, D), 1.0, 6.0, ((0, 8),), (0, 1, 8, 2.0))
    cotangent = bell_draw_with(key_of[1], (TOKENS, D), 1.0, 6.0, ((0, 8),), (0, 1, 8, 2.0))
    norm_gain = jnp.clip(1.0 + 0.1 * jax.random.normal(key_of[2], (D,), jnp.float32), 0.5, 1.5)
    w_x = scatter_about(key_of[3], (D, NH, HD), D ** -0.5, 0.1875, ((0, 8), (1, 2), (2, 2)))
    w_z = scatter_about(key_of[4], (D, NH, HD), D ** -0.5, 0.1875, ((0, 8), (1, 2), (2, 2)))
    w_bc = scatter_about(key_of[5], (D, 2, N), D ** -0.5, 0.1875, ((0, 8),))
    w_dt = scatter_about(key_of[6], (D, NH), D ** -0.5, 0.1875, ((0, 8), (1, 2)))
    conv_x = scatter_about(key_of[7], (NH, HD, K), K ** -0.5, 3.0, ((0, 2), (1, 2)), jnp.float32)
    conv_bc = scatter_about(key_of[8], (2, N, K), K ** -0.5, 3.0, (), jnp.float32)
    dt_bias = jnp.clip(-6.0 + 4.0 * jax.random.uniform(key_of[9], (NH,), jnp.float32) ** level_of(key_of[9], (NH,), ((0, 2),), -0.2, 0.2), -6.0, -2.0)
    a_log = jnp.clip(-1.5 + 2.0 * jax.random.uniform(key_of[10], (NH,), jnp.float32) ** level_of(key_of[10], (NH,), ((0, 2),), -0.2, 0.2), -1.5, 0.5)
    skip = jnp.clip(0.5 + 1.0 * jax.random.uniform(key_of[11], (NH,), jnp.float32) ** level_of(key_of[11], (NH,), ((0, 2),), -0.2, 0.2), 0.5, 1.5)
    gate_gain = jnp.clip(1.0 + 0.1 * jax.random.normal(key_of[12], (NH, HD), jnp.float32), 0.5, 1.5)
    w_out = scatter_about(key_of[13], (NH, HD, D), DI ** -0.5, 0.125, ((0, 2), (1, 2), (2, 8)))
    return {"block_in": block_in, "cotangent": cotangent, "norm_gain": norm_gain, "w_x": w_x, "w_z": w_z, "w_bc": w_bc, "w_dt": w_dt, "conv_x": conv_x, "conv_bc": conv_bc, "dt_bias": dt_bias, "a_log": a_log, "skip": skip, "gate_gain": gate_gain, "w_out": w_out}


EPSILON = 1e-05
PRECISE = lax.Precision.HIGHEST

def causal_conv(signal, kernel):
    taps = kernel.shape[1]
    length = signal.shape[0]
    padded = jnp.pad(signal, ((taps - 1, 0), (0, 0)))
    total = jnp.zeros_like(signal)
    for offset in range(taps):
        total = total + padded[offset:offset + length] * kernel[:, offset]
    return total

def conv_silu(signal, kernel):
    return jax.nn.silu(causal_conv(signal, kernel))

def silu_slope(value):
    sigma = jax.nn.sigmoid(value)
    return sigma * (1.0 + value * (1.0 - sigma))

def scan_spans(values, step_size, rate, b_maps, c_maps, block):
    length, head_count, channels = values.shape
    blocks = length // block
    logs = (step_size * rate).reshape(blocks, block, head_count)
    cums = jnp.cumsum(logs, axis=1)
    x_blocks = values.reshape(blocks, block, head_count, channels)
    dt_blocks = step_size.reshape(blocks, block, head_count)
    b_blocks = b_maps.reshape(blocks, block, -1)
    c_blocks = c_maps.reshape(blocks, block, -1)
    scores = jnp.einsum('cln,csn->cls', c_blocks, b_blocks, precision=PRECISE)
    causal = (jnp.arange(block)[:, None] >= jnp.arange(block)[None, :])[None, :, :, None]
    gaps = cums[:, :, None, :] - cums[:, None, :, :]
    decays = jnp.where(causal, jnp.exp(jnp.where(causal, gaps, 0.0)), 0.0)
    mixing = scores[..., None] * decays * dt_blocks[:, None, :, :]
    intra_part = jnp.einsum('clsh,cshp->clhp', mixing, x_blocks, precision=PRECISE)
    to_end = jnp.exp(cums[:, -1:, :] - cums) * dt_blocks
    states = jnp.einsum('csh,csn,cshp->chpn', to_end, b_blocks, x_blocks, precision=PRECISE)
    whole_decay = jnp.exp(cums[:, -1, :])
    carried = []
    running = jnp.zeros_like(states[0])
    for position in range(blocks):
        carried.append(running)
        running = running * whole_decay[position][:, None, None] + states[position]
    entering = jnp.stack(carried)
    inter_part = jnp.einsum('cln,clh,chpn->clhp', c_blocks, jnp.exp(cums), entering, precision=PRECISE)
    return (intra_part + inter_part).reshape(length, head_count, channels)

def mixer(values, dt_raw, dt_bias, a_log, skip, b_maps, c_maps, block):
    step_size = jax.nn.softplus(dt_raw + dt_bias)
    rate = -jnp.exp(a_log)
    return scan_spans(values, step_size, rate, b_maps, c_maps, block) + skip[:, None] * values

def one_sequence(params, rows_in, upstream_bf):
    norm_gain, w_x, w_z, w_bc, w_dt, conv_x, conv_bc, dt_bias, a_log, skip, gate_gain, w_out = params
    inner_width = NH * HD
    weight_x = w_x.reshape(D, inner_width)
    weight_z = w_z.reshape(D, inner_width)
    weight_bc = w_bc.reshape(D, 2 * N)
    weight_out = w_out.reshape(inner_width, D)
    kernel_x = conv_x.reshape(inner_width, K)
    kernel_bc = conv_bc.reshape(2 * N, K)
    gain_flat = gate_gain.reshape(inner_width)
    features = rows_in.astype(jnp.float32)
    scale_in = lax.rsqrt(lax.optimization_barrier(jnp.mean(features * features, axis=1, keepdims=True)) + EPSILON)
    normed = (features * scale_in * norm_gain).astype(jnp.bfloat16)
    x_raw = jnp.dot(normed, weight_x, preferred_element_type=jnp.float32)
    z_raw = jnp.dot(normed, weight_z, preferred_element_type=jnp.float32)
    bc_raw = jnp.dot(normed, weight_bc, preferred_element_type=jnp.float32)
    dt_raw = jnp.dot(normed, w_dt, preferred_element_type=jnp.float32)
    x_act = conv_silu(x_raw, kernel_x).astype(jnp.bfloat16)
    bc_act = conv_silu(bc_raw, kernel_bc).astype(jnp.bfloat16)
    values = x_act.astype(jnp.float32).reshape(LEN, NH, HD)
    b_maps = bc_act[:, :N].astype(jnp.float32)
    c_maps = bc_act[:, N:].astype(jnp.float32)
    mixed = mixer(values, dt_raw, dt_bias, a_log, skip, b_maps, c_maps, SPAN).reshape(LEN, inner_width)
    gated = mixed * jax.nn.silu(z_raw)
    scale_out = lax.rsqrt(lax.optimization_barrier(jnp.sum(gated * gated, axis=1, keepdims=True)) / inner_width + EPSILON)
    normed_out = (gated * scale_out * gain_flat).astype(jnp.bfloat16)
    block_out = (jnp.dot(normed_out, weight_out, preferred_element_type=jnp.float32) + features).astype(jnp.bfloat16)
    upstream = upstream_bf.astype(jnp.float32)
    d_normed_out = jnp.dot(upstream_bf, weight_out.T, preferred_element_type=jnp.float32)
    g_w_out = jnp.dot(normed_out.T, upstream_bf, preferred_element_type=jnp.float32)
    g_gate_gain = lax.optimization_barrier(jnp.sum(d_normed_out * gated * scale_out, axis=0))
    d_hat = d_normed_out * gain_flat
    inner_sum = lax.optimization_barrier(jnp.sum(d_hat * gated, axis=1, keepdims=True))
    d_gated = scale_out * d_hat - gated * scale_out ** 3 * inner_sum / inner_width
    d_mixed = d_gated * jax.nn.silu(z_raw)
    d_z = (d_gated * mixed * silu_slope(z_raw)).astype(jnp.bfloat16)
    _, pullback = jax.vjp(partial(mixer, block=SPAN), values, dt_raw, dt_bias, a_log, skip, b_maps, c_maps)
    d_xs, d_dt, g_dt_bias, g_a_log, g_skip, d_b, d_c = pullback(d_mixed.reshape(LEN, NH, HD))
    _, pull_x = jax.vjp(conv_silu, x_raw, kernel_x)
    d_x_raw, g_conv_x = pull_x(d_xs.reshape(LEN, inner_width))
    _, pull_bc = jax.vjp(conv_silu, bc_raw, kernel_bc)
    d_bc_raw, g_conv_bc = pull_bc(jnp.concatenate([d_b, d_c], axis=1))
    d_x_b = d_x_raw.astype(jnp.bfloat16)
    d_bc_b = d_bc_raw.astype(jnp.bfloat16)
    d_dt_b = d_dt.astype(jnp.bfloat16)
    g_w_x = jnp.dot(normed.T, d_x_b, preferred_element_type=jnp.float32)
    g_w_z = jnp.dot(normed.T, d_z, preferred_element_type=jnp.float32)
    g_w_bc = jnp.dot(normed.T, d_bc_b, preferred_element_type=jnp.float32)
    g_w_dt = jnp.dot(normed.T, d_dt_b, preferred_element_type=jnp.float32)
    d_normed = jnp.dot(d_x_b, weight_x.T, preferred_element_type=jnp.float32) + jnp.dot(d_z, weight_z.T, preferred_element_type=jnp.float32) + jnp.dot(d_dt_b, w_dt.T, preferred_element_type=jnp.float32) + jnp.dot(d_bc_b, weight_bc.T, preferred_element_type=jnp.float32)
    g_norm_gain = lax.optimization_barrier(jnp.sum(d_normed * features * scale_in, axis=0))
    d_in_hat = d_normed * norm_gain
    grad_in = scale_in * d_in_hat - features * scale_in ** 3 * lax.optimization_barrier(jnp.mean(d_in_hat * features, axis=1, keepdims=True)) + upstream
    grads = (g_norm_gain, g_w_x.reshape(D, NH, HD), g_w_z.reshape(D, NH, HD), g_w_bc.reshape(D, 2, N), g_w_dt, g_conv_x.reshape(NH, HD, K), g_conv_bc.reshape(2, N, K), g_dt_bias, g_a_log, g_skip, g_gate_gain.reshape(NH, HD), g_w_out.reshape(NH, HD, D))
    return (block_out, grad_in, grads)

def reference(block_in, cotangent, norm_gain, w_x, w_z, w_bc, w_dt, conv_x, conv_bc, dt_bias, a_log, skip, gate_gain, w_out):
    params = (norm_gain, w_x, w_z, w_bc, w_dt, conv_x, conv_bc, dt_bias, a_log, skip, gate_gain, w_out)
    start = tuple((jnp.zeros(leaf.shape, jnp.float32) for leaf in params))

    def step_fn(totals, pair):
        out_rows, grad_rows, grads = one_sequence(params, pair[0], pair[1])
        return (tuple((a + b for a, b in zip(totals, grads))), (out_rows, grad_rows))
    totals, stacked = lax.scan(step_fn, start, (block_in.reshape(SEQS, LEN, D), cotangent.reshape(SEQS, LEN, D)))
    block_out = stacked[0].reshape(TOKENS, D)
    grad_in = stacked[1].reshape(TOKENS, D)
    return (block_out, grad_in, totals[0], totals[1], totals[2], totals[3], totals[4], totals[5], totals[6], totals[7], totals[8], totals[9], totals[10], totals[11])
```

```python
from functools import partial
from types import SimpleNamespace

import jax
import jax.numpy as jnp
from jax import lax
from jax.experimental import pallas as pl
from jax.experimental.pallas import tpu as pltpu
from jax.sharding import PartitionSpec as P

EPSILON = 1e-05
PRECISE = lax.Precision.HIGHEST
LANES = 128
SPAN = 128
ROWS = 32
PIECES = 2
LATE_Z = 2
LATE_OUT = 4
VMEM_LIMIT = 60 * 1024 * 1024
MESH = pl.DeviceIdType.MESH
VMEM_SPEC = pl.BlockSpec(memory_space=pltpu.VMEM)
LOW = jnp.bfloat16
FULL = jnp.float32


def ring_index(position, count):
    high = position // (count // 2)
    return (1 - high) * 2 * position + high * (2 * (count - 1 - position) + 1)


def ring_position(index, count):
    odd = index % 2
    return (1 - odd) * (index // 2) + odd * (count - 1 - index // 2)


def last_axes(a, b):
    return lax.dot_general(a, b, (((1,), (1,)), ((), ())), preferred_element_type=FULL)


def first_axes(a, b):
    return lax.dot_general(a, b, (((0,), (0,)), ((), ())), preferred_element_type=FULL)


def plain(a, b):
    return jnp.dot(a, b, preferred_element_type=FULL)


def high_low(value):
    high = value.astype(LOW)
    return high, (value - high.astype(FULL)).astype(LOW)


def sigmoid(value):
    return 1.0 / (1.0 + jnp.exp(-value))


def silu_slope(value, sigma):
    return sigma * (1.0 + value * (1.0 - sigma))


def softplus(value):
    return jnp.maximum(value, 0.0) + jnp.log1p(jnp.exp(-jnp.abs(value)))


def later(rows, amount):
    if amount == 0:
        return rows
    lane = lax.broadcasted_iota(jnp.int32, rows.shape, 1)
    return jnp.where(lane >= amount, pltpu.roll(rows, amount, 1), 0.0)


def sooner(rows, amount):
    if amount == 0:
        return rows
    length = rows.shape[1]
    lane = lax.broadcasted_iota(jnp.int32, rows.shape, 1)
    return jnp.where(lane < length - amount, pltpu.roll(rows, length - amount, 1), 0.0)


def own_lanes(hc, hw):
    shape = (hc, hc * hw)
    first = lax.broadcasted_iota(jnp.int32, shape, 0) * hw
    lane = lax.broadcasted_iota(jnp.int32, shape, 1)
    return (lane >= first) & (lane < first + hw)


def lane_places(hc, hw):
    shape = (hw, hc * hw)
    lane = lax.broadcasted_iota(jnp.int32, shape, 1)
    place = lax.broadcasted_iota(jnp.int32, shape, 0)
    return jnp.where(jnp.bitwise_and(lane, hw - 1) == place, 1.0, 0.0)


def group_peers(heads, tensors):
    head, tensor = lax.axis_index("head"), lax.axis_index("tensor")
    peers = []
    for offset in range(1, heads * tensors):
        peer_head = (head + offset // tensors) % heads
        peer_tensor = (tensor + offset % tensors) % tensors
        peers.append((peer_head, peer_tensor))
    return head * tensors + tensor, peers


class Block:

    def __init__(self, count, rows):
        self.count, self.rows = count, rows
        self.turned = rows % LANES == 0

    def shape(self, columns):
        return (columns, self.rows) if self.turned else (self.rows, columns)

    def halves(self, ref):
        unit = 16 if self.turned else LANES
        columns = ref.shape[0] if self.turned else ref.shape[1]
        first = (columns // unit + 1) // 2 * unit
        starts = [(0, first), (first, columns - first)] if first < columns else [(0, first)]
        return [self.slice(*start) for start in starts]

    def slice(self, start, amount):
        part = pl.ds(start, amount)
        return (part, slice(None)) if self.turned else (slice(None), part)

    def sizes(self, columns):
        shape = jax.ShapeDtypeStruct(self.shape(columns), LOW)
        return [
            (cut[0].size, self.rows) if self.turned else (self.rows, cut[1].size)
            for cut in self.halves(shape)
        ]

    def matrix(self, ref):
        if self.turned:
            return jnp.concatenate([ref[i] for i in range(self.count)], axis=1)
        return ref[...].reshape(self.count * self.rows, ref.shape[2])

    def project(self, a, matrix):
        return last_axes(a, matrix) if self.turned else plain(a, matrix)

    def back(self, a, matrix):
        return plain(a, matrix) if self.turned else last_axes(a, matrix)

    def store(self, ref, matrix):
        if self.turned:
            for i in range(self.count):
                ref[i] = matrix[:, i * self.rows : (i + 1) * self.rows].astype(ref.dtype)
        else:
            ref[...] = matrix.reshape(ref.shape).astype(ref.dtype)

    def gradient(self, act_ref, d_ref, out_ref):
        if self.turned:
            d = d_ref[...]
            for i in range(self.count):
                part = act_ref[:, i * self.rows : (i + 1) * self.rows]
                out_ref[i] = first_axes(d, part).astype(out_ref.dtype)
        else:
            self.store(out_ref, first_axes(act_ref[...], d_ref[...]))


def block_kernel(dims, names, sem_names, *args):
    ref = SimpleNamespace(**dict(zip(names, args)))
    pairs = args[len(names) :]
    sem = SimpleNamespace(
        **{name: (pairs[2 * i], pairs[2 * i + 1]) for i, name in enumerate(sem_names)}
    )
    count, heads, tensors, hw, taps, state, quarter = (
        dims[k] for k in ("count", "heads", "tensors", "hw", "taps", "state", "quarter")
    )
    T, D = ref.x_in.shape
    hc = ref.skip.shape[1]
    I = hc * hw
    size = heads * tensors
    block = dims["block"]
    side_rows = dims["side_rows"]
    groups = I // LANES
    per = LANES // hw
    spans = T // SPAN
    head, tensor = lax.axis_index("head"), lax.axis_index("tensor")
    me = lax.axis_index("fsdp")
    group_me, peers = group_peers(heads, tensors)
    position = ring_position(me, count)
    right = ring_index((position + 1) % count, count)
    left = ring_index((position + count - 1) % count, count)
    others = [(me + offset) % count for offset in range(1, count)]
    head_peers = [(head + offset) % heads for offset in range(1, heads)]
    tensor_peers = [(tensor + offset) % tensors for offset in range(1, tensors)]
    started = []

    barrier = pltpu.get_barrier_semaphore()
    for h, t in peers:
        pl.semaphore_signal(barrier, inc=1, device_id={"head": h, "tensor": t}, device_id_type=MESH)
    for other in others:
        pl.semaphore_signal(barrier, inc=1, device_id={"fsdp": other}, device_id_type=MESH)
    pl.semaphore_wait(barrier, len(peers) + len(others))

    def send(source, target, sems, place, device):
        copy = pltpu.make_async_remote_copy(
            src_ref=source,
            dst_ref=target,
            send_sem=sems[0].at[place],
            recv_sem=sems[1].at[place],
            device_id=device,
            device_id_type=MESH,
        )
        copy.start()
        started.append(copy)
        return copy

    half_count = count // 2
    rights = [ring_index((position + count - i) % count, count) for i in range(half_count + 1)]
    lefts = [ring_index((position + i) % count, count) for i in range(half_count + 1)]

    def gather_part(shard, full, sems):
        cuts = block.halves(shard)
        full[me] = shard[...]
        copies = {}

        def step_at(step):
            for way, cut in enumerate(cuts):
                for turn, (target, owners) in enumerate(((right, rights), (left, lefts))):
                    if step > 0 and (step < half_count or way == turn):
                        copies[way, turn, step - 1].wait_recv()
                    if step < half_count - 1 or (step == half_count - 1 and way == turn):
                        place = full.at[(owners[step],) + cut]
                        source = shard.at[cut] if step == 0 else place
                        copies[way, turn, step] = send(
                            source, place, sems, (way, turn, step), {"fsdp": target}
                        )

        return step_at

    def scatter_part(grads, own, slots, sems):
        cuts = block.halves(own)
        copies = {}

        def step_at(step):
            for way, cut in enumerate(cuts):
                held = slots[way]
                if step == half_count:
                    total = grads[(me,) + cut].astype(FULL)
                    for turn in range(2):
                        copies[way, turn, step - 1].wait_recv()
                        total = total + held[turn, step - 1].astype(FULL)
                    own[cut] = total
                    continue
                for turn, (target, owners) in enumerate(((right, lefts), (left, rights))):
                    piece = (owners[half_count - step],) + cut
                    if step == 0 and way != turn:
                        continue
                    if step == 0 or (step == 1 and way != turn):
                        source = grads.at[piece]
                    else:
                        copies[way, turn, step - 1].wait_recv()
                        total = held[turn, step - 1].astype(FULL) + grads[piece].astype(FULL)
                        held[turn, step - 1] = total.astype(LOW)
                        source = held.at[turn, step - 1]
                    copies[way, turn, step] = send(
                        source, held.at[turn, step], sems, (way, turn, step), {"fsdp": target}
                    )

        return step_at

    def rounds(parts):
        keyed = [
            (late + step, place, step_at, step)
            for place, (late, step_at) in enumerate(parts)
            for step in range(half_count + 1)
        ]
        keyed.sort(key=lambda entry: entry[:2])
        return keyed

    queue = []

    def pump(amount):
        for _ in range(amount):
            if queue:
                key = queue[0][0]
                while queue and queue[0][0] == key:
                    _, _, step_at, step = queue.pop(0)
                    step_at(step)

    def pump_until(key):
        while queue and queue[0][0] <= key:
            pump(1)

    def row_loop(body, first=0, last=T):
        def run(i, carry):
            body(pl.multiple_of(first + i * ROWS, ROWS))
            return carry

        lax.fori_loop(0, (last - first) // ROWS, run, 0)

    queue += rounds(
        [
            (0, gather_part(ref.wx, ref.all_x, sem.gather_x)),
            (0, lambda step: side_part[0](step)),
            (LATE_Z, gather_part(ref.wz, ref.all_z, sem.gather_z)),
            (LATE_OUT, gather_part(ref.wo, ref.all_o, sem.gather_o)),
        ]
    )
    queue.pop(0)[2](0)
    maps = ref.w_bc[...].astype(FULL).T
    ref.maps[...] = maps
    mine_at = pl.ds(pl.multiple_of(group_me * quarter, quarter), quarter)
    side_list = [ref.maps[mine_at, :], ref.w_dt[...].astype(FULL)]
    if side_rows > quarter + hc:
        side_list.append(jnp.zeros((side_rows - quarter - hc, maps.shape[1]), FULL))
    side = jnp.concatenate(side_list, axis=0)
    ref.ws[...] = (side if block.turned else side.T).astype(LOW)
    side_part = [gather_part(ref.ws, ref.all_s, sem.gather_s)]
    pump(1)

    def norm_rows(r):
        at = pl.ds(r, ROWS)
        features = ref.x_in[at, :].astype(FULL)
        mean = jnp.mean(features * features, axis=1, keepdims=True)
        scale = lax.rsqrt(mean + EPSILON)
        ref.scale_in[at, :] = scale
        ref.normed[at, :] = (features * scale * ref.norm_gain[...]).astype(LOW)

    row_loop(norm_rows)
    ref.x_pad[0:8, :] = jnp.zeros((8, I), FULL)
    ref.d_conv[T : T + 8, :] = jnp.zeros((8, I), FULL)
    ref.columns[...] = jnp.zeros((T, LANES), FULL)
    ref.sums[...] = jnp.zeros((8, I), FULL)

    ours = own_lanes(hc, hw)
    place_of = lane_places(hc, hw)
    equal = lax.broadcasted_iota(jnp.int32, (hc, hc), 0) == lax.broadcasted_iota(
        jnp.int32, (hc, hc), 1
    )

    def column(row_ref):
        return jnp.sum(jnp.where(equal, row_ref[...], 0.0), axis=1, keepdims=True)

    def spread(by_head):
        wide = jnp.dot(by_head, place_of, precision=PRECISE, preferred_element_type=FULL)
        return jnp.sum(jnp.where(ours, wide, 0.0), axis=0, keepdims=True)

    for k in range(taps):
        ref.kernel_x[k : k + 1, :] = spread(ref.conv_x[:, k, :])
    ref.gain[...] = spread(ref.gate_gain[...])
    ref.skip_wide[...] = jnp.sum(jnp.where(ours, column(ref.skip), 0.0), axis=0, keepdims=True)
    ref.kernel_all[...] = jnp.concatenate([ref.conv_bc[i].T for i in range(2)], axis=0)
    ref.kernel_bc[...] = ref.kernel_all[mine_at, :]
    expand = jnp.where(ours, 1.0, 0.0).astype(LOW)
    expand_two = jnp.concatenate([expand, expand], axis=0)

    def widen(rows):
        return first_axes(jnp.concatenate(high_low(rows), axis=0), expand_two)

    def narrow(wide):
        high, low = high_low(wide)
        return last_axes(expand, high) + last_axes(expand, low)

    pump_until(half_count)

    normed = ref.normed
    if block.turned:
        side = last_axes(block.matrix(ref.all_s), normed[...])
    else:
        side = plain(normed[...], block.matrix(ref.all_s)).T
    bc_raw = side[0:quarter]
    ref.bc_raw[...] = bc_raw
    kernel_bc = ref.kernel_bc
    bc_conv = sum(later(bc_raw, taps - 1 - k) * kernel_bc[:, k : k + 1] for k in range(taps))
    ref.bc_conv[...] = bc_conv
    ref.bc_mine[...] = (bc_conv * sigmoid(bc_conv)).astype(LOW)
    bc = ref.bc
    bc_copies = [
        send(ref.bc_mine, bc.at[mine_at, :], sem.bc, place, {"head": h, "tensor": t})
        for place, (h, t) in enumerate(peers)
    ]
    bc[mine_at, :] = ref.bc_mine[...]

    half = T // 2
    x_matrix = block.matrix(ref.all_x)
    for first in (0, half):
        ref.x_pad[8 + first : 8 + first + half, :] = block.project(
            normed[first : first + half, :], x_matrix
        )
        pump(1)

    dt_in = side[quarter : quarter + hc] + column(ref.dt_bias)
    step = softplus(dt_in)
    rate = -jnp.exp(column(ref.a_log))
    logs = step * rate
    ref.dt_in[...] = dt_in
    ref.step[...] = step
    sooner_row = lax.broadcasted_iota(jnp.int32, (SPAN, SPAN), 0)
    later_lane = lax.broadcasted_iota(jnp.int32, (SPAN, SPAN), 1)
    upper = jnp.where(sooner_row <= later_lane, 1.0, 0.0)
    lower = jnp.where(sooner_row >= later_lane, 1.0, 0.0)
    causal = sooner_row >= later_lane
    cums, to_end = [], []
    for c in range(spans):
        part = jnp.dot(
            logs[:, c * SPAN : (c + 1) * SPAN], upper, precision=PRECISE, preferred_element_type=FULL
        )
        cums.append(part)
        to_end.append(part[:, SPAN - 1 : SPAN] - part)
    cums = jnp.concatenate(cums, axis=1)
    ref.cums[...] = cums
    ref.cum_columns[...] = cums.T
    ref.from_start[...] = widen(jnp.exp(cums))
    ref.to_end[...] = widen(jnp.exp(jnp.concatenate(to_end, axis=1)))
    ref.step_wide[...] = widen(step)
    pump(1)

    kernel_x = ref.kernel_x

    def conv_rows(r):
        at = pl.ds(r, ROWS)
        near = ref.x_pad[pl.ds(r, ROWS + 8), :]
        conv = sum(
            kernel_x[k : k + 1, :] * near[9 - taps + k : 9 - taps + k + ROWS] for k in range(taps)
        )
        ref.conv[at, :] = conv
        act = (conv * sigmoid(conv)).astype(LOW)
        ref.act[at, :] = act
        v = act.astype(FULL) * ref.step_wide[at, :]
        ref.v[at, :] = v.astype(LOW)
        ref.v_end[at, :], ref.v_end_low[at, :] = high_low(v * ref.to_end[at, :])

    row_loop(conv_rows)
    pump(1)
    for copy in bc_copies:
        copy.wait_recv()

    head_lane = lax.broadcasted_iota(jnp.int32, (SPAN, LANES), 1)
    lanes_of = [(head_lane >= i * hw) & (head_lane < (i + 1) * hw) for i in range(per)]

    def maps_of(c):
        at = slice(c * SPAN, (c + 1) * SPAN)
        return bc[0:state, at], bc[state : 2 * state, at]

    def decay_of(c, h):
        at = slice(c * SPAN, (c + 1) * SPAN)
        gap = ref.cum_columns[at, h : h + 1] - ref.cums[h : h + 1, at]
        return jnp.exp(jnp.where(causal, gap, -1e30))

    y = ref.y
    for c in range(spans):
        at = slice(c * SPAN, (c + 1) * SPAN)
        b_map, c_map = maps_of(c)
        scores = first_axes(c_map, b_map)
        if c > 0:
            y[at, :] = (first_axes(c_map, ref.states[c]) + first_axes(c_map, ref.states_low[c])) * ref.from_start[at, :]
        for g in range(groups):
            lanes = slice(g * LANES, (g + 1) * LANES)
            v = ref.v[at, lanes]
            weights, values = [], []
            for i in range(per):
                weights.append((scores * decay_of(c, g * per + i)).astype(LOW))
                values.append(jnp.where(lanes_of[i], v, jnp.zeros_like(v)))
            part = plain(jnp.concatenate(weights, axis=1), jnp.concatenate(values, axis=0))
            y[at, lanes] = part if c == 0 else y[at, lanes] + part
        if c + 1 < spans:
            new = plain(b_map, ref.v_end[at, :]) + plain(b_map, ref.v_end_low[at, :])
            if c > 0:
                whole = ref.from_start[(c + 1) * SPAN - 1 : (c + 1) * SPAN, :]
                new = ref.running[...] * whole + new
            ref.running[...] = new
            ref.states[c + 1], ref.states_low[c + 1] = high_low(new)
        pump(1)

    pump_until(LATE_Z + half_count)
    z_matrix = block.matrix(ref.all_z)
    for first in (0, half):
        ref.z[first : first + half, :] = block.project(normed[first : first + half, :], z_matrix)
    pump(1)
    skip = ref.skip_wide
    gain = ref.gain
    columns = ref.columns

    def gate_rows(r):
        at = pl.ds(r, ROWS)
        z = ref.z[at, :]
        mixed = y[at, :] + skip[...] * ref.act[at, :].astype(FULL)
        gated = mixed * (z * sigmoid(z))
        ref.gated[at, :] = gated
        columns[at, 0:1] = jnp.sum(gated * gated, axis=1, keepdims=True)

    row_loop(gate_rows)
    pump_until(LATE_OUT + half_count)

    o_matrix = block.matrix(ref.all_o)
    for first in (0, half):
        ref.d_no[first : first + half, :] = block.project(
            ref.cot[first : first + half, :], o_matrix
        )

    def inner_rows(r):
        at = pl.ds(r, ROWS)
        columns[at, 1:2] = jnp.sum(
            ref.d_no[at, :] * gain[...] * ref.gated[at, :], axis=1, keepdims=True
        )

    row_loop(inner_rows)
    ref.pair[...] = columns[...].T[0:8]
    ref.pairs[group_me] = ref.pair[...]
    pair_copies = [
        send(ref.pair, ref.pairs.at[group_me], sem.pair, place, {"head": h, "tensor": t})
        for place, (h, t) in enumerate(peers)
    ]
    for copy in pair_copies:
        copy.wait_recv()
    pair = ref.pairs[0]
    for k in range(1, size):
        pair = pair + ref.pairs[k]
    full_inner = I * size
    scale_row = lax.rsqrt(pair[0:1] / full_inner + EPSILON)
    third_row = scale_row * scale_row * scale_row * (pair[1:2] / full_inner)
    fill = jnp.zeros((6, T), FULL)
    ref.scales[...] = jnp.concatenate([scale_row, third_row, fill], axis=0).T

    def gate_back_rows(r):
        at = pl.ds(r, ROWS)
        scale = ref.scales[at, 0:1]
        third = ref.scales[at, 1:2]
        gated, d_no, z = ref.gated[at, :], ref.d_no[at, :], ref.z[at, :]
        act = ref.act[at, :].astype(FULL)
        hat = gated * scale
        ref.normed_out[at, :] = (hat * gain[...]).astype(LOW)
        d_gated = scale * (d_no * gain[...]) - gated * third
        sigma = sigmoid(z)
        d_mixed = d_gated * (z * sigma)
        mixed = y[at, :] + skip[...] * act
        ref.d_z[at, :] = (d_gated * mixed * silu_slope(z, sigma)).astype(LOW)
        ref.d_mixed[at, :] = d_mixed
        ref.dy[at, :] = d_mixed.astype(LOW)
        ref.dy_start[at, :], ref.dy_start_low[at, :] = high_low(d_mixed * ref.from_start[at, :])
        ref.sums[0:1, :] += jnp.sum(d_no * hat, axis=0, keepdims=True)
        ref.sums[1:2, :] += jnp.sum(d_mixed * act, axis=0, keepdims=True)

    row_loop(gate_back_rows)

    queue.clear()
    scatter_o = scatter_part(ref.g_o, ref.own_o, (ref.slot_o0, ref.slot_o1), sem.scatter_o)
    scatter_z = scatter_part(ref.g_z, ref.own_z, (ref.slot_z0, ref.slot_z1), sem.scatter_z)
    scatter_x = scatter_part(ref.g_x, ref.own_x, (ref.slot_x0, ref.slot_x1), sem.scatter_x)
    scatter_s = scatter_part(ref.g_s, ref.own_s, (ref.slot_s0, ref.slot_s1), sem.scatter_s)
    block.gradient(ref.cot, ref.normed_out, ref.g_o)
    scatter_o(0)
    block.gradient(normed, ref.d_z, ref.g_z)
    scatter_z(0)
    queue += [
        (step, place, step_at, step)
        for step in range(1, half_count + 1)
        for place, step_at in enumerate((scatter_o, scatter_z))
    ]

    share = T // heads
    piece = share // PIECES

    class GroupSum:
        def __init__(self, source, result, finish, held, sems):
            self.source, self.result, self.finish = source, result, finish
            self.by_head, self.middle, self.by_tensor = held
            self.sems = sems
            self.from_head, self.from_tensor, self.back = {}, {}, {}

        def rows(self, h, j):
            return pl.ds(pl.multiple_of(h * share + j * piece, piece), piece)

        def start(self, j):
            self.from_head[j] = [
                send(
                    self.source.at[self.rows(peer, j), :], self.by_head.at[j, k], self.sems[0],
                    (j, k), {"head": peer},
                )
                for k, peer in enumerate(head_peers)
            ]

        def across(self, j):
            for copy in self.from_head[j]:
                copy.wait_recv()
            total = self.source[self.rows(head, j), :].astype(FULL)
            for k in range(heads - 1):
                total = total + self.by_head[j, k].astype(FULL)
            total = total.astype(LOW)
            self.middle[j] = total
            self.by_tensor[j, tensor] = total
            self.from_tensor[j] = [
                send(
                    self.middle.at[j], self.by_tensor.at[j, tensor], self.sems[1], (j, k),
                    {"tensor": peer},
                )
                for k, peer in enumerate(tensor_peers)
            ]

        def close(self, j):
            for copy in self.from_tensor[j]:
                copy.wait_recv()
            total = self.by_tensor[j, 0].astype(FULL)
            for k in range(1, tensors):
                total = total + self.by_tensor[j, k].astype(FULL)
            at = self.rows(head, j)
            self.result[at, :] = self.finish(at, total).astype(LOW)
            self.back[j] = [
                send(
                    self.result.at[at, :], self.result.at[at, :], self.sems[2], (j, k),
                    {"head": peer},
                )
                for k, peer in enumerate(head_peers)
            ]

        def end(self):
            for j in range(PIECES):
                for copy in self.back[j]:
                    copy.wait_recv()

    def finish_out(at, total):
        return total + ref.x_in[at, :].astype(FULL)

    norm_gain = ref.norm_gain

    def finish_in(at, total):
        features = ref.x_in[at, :].astype(FULL)
        scale = ref.scale_in[at, :]
        ref.norm_sum[0:1, :] += jnp.sum(total * (features * scale), axis=0, keepdims=True)
        inner = total * norm_gain[...]
        mean = jnp.mean(inner * features, axis=1, keepdims=True)
        return scale * inner - features * (scale * scale * scale * mean)

    out_sum = GroupSum(
        ref.partial_out, ref.block_out, finish_out, (ref.out_a, ref.out_m, ref.out_b),
        (sem.out_a, sem.out_b, sem.out_c),
    )
    in_sum = GroupSum(
        ref.partial_in, ref.low_in, finish_in, (ref.in_a, ref.in_m, ref.in_b),
        (sem.in_a, sem.in_b, sem.in_c),
    )
    for first in (0, half):
        ref.partial_out[first : first + half, :] = block.back(
            ref.normed_out[first : first + half, :], o_matrix
        ).astype(LOW)
    for j in range(PIECES):
        out_sum.start(j)

    d_bc = ref.d_bc
    d_row = []
    for c in reversed(range(spans)):
        at = slice(c * SPAN, (c + 1) * SPAN)
        b_map, c_map = maps_of(c)
        scores = first_axes(c_map, b_map)
        d_scores = jnp.zeros((SPAN, SPAN), FULL)
        last = c + 1 == spans
        if not last:
            low_d_state, lower_d_state = high_low(ref.d_state[...])
            ref.u[at, :] = (first_axes(b_map, low_d_state) + first_axes(b_map, lower_d_state)) * ref.to_end[at, :]
        for g in range(groups):
            lanes = slice(g * LANES, (g + 1) * LANES)
            v = ref.v[at, lanes]
            dy = ref.dy[at, lanes]
            dy_turned = dy.astype(FULL).T.astype(LOW)
            lane_row = lax.broadcasted_iota(jnp.int32, (LANES, SPAN), 0)
            weights, values = [], []
            for i in range(per):
                decay = decay_of(c, g * per + i)
                weights.append((scores * decay).astype(LOW))
                mine = (lane_row >= i * hw) & (lane_row < (i + 1) * hw)
                values.append(jnp.where(mine, dy_turned, jnp.zeros_like(dy_turned)))
                own_dy = jnp.where(lanes_of[i], dy, jnp.zeros_like(dy))
                d_scores = d_scores + last_axes(own_dy, v) * decay
            part = plain(jnp.concatenate(values, axis=1), jnp.concatenate(weights, axis=0)).T
            ref.u[at, lanes] = part if last else ref.u[at, lanes] + part
        low_d = d_scores.astype(LOW)
        d_b = plain(c_map, low_d)
        d_c = last_axes(b_map, low_d)
        if not last:
            d_b = d_b + last_axes(low_d_state, ref.v_end[at, :])
        if c > 0:
            d_c = d_c + last_axes(ref.states[c], ref.dy_start[at, :])
        d_bc[0:state, at] = d_b.astype(LOW)
        d_bc[state : 2 * state, at] = d_c.astype(LOW)

        u = ref.u[at, :]
        balance = narrow(
            ref.dy[at, :].astype(FULL) * y[at, :] - ref.v[at, :].astype(FULL) * u
        )
        d_logs = jnp.dot(balance, lower, precision=PRECISE, preferred_element_type=FULL)
        if not last:
            passed = jnp.sum(
                (ref.states[c + 1].astype(FULL) + ref.states_low[c + 1].astype(FULL)) * ref.d_state[...], axis=0, keepdims=True
            )
            passed = jnp.sum(jnp.where(ours, passed, 0.0), axis=1, keepdims=True)
            d_logs = d_logs + passed
        d_step = narrow(ref.act[at, :].astype(FULL) * u)
        d_row.append((d_logs, d_step))
        if c > 0:
            new = plain(c_map, ref.dy_start[at, :]) + plain(c_map, ref.dy_start_low[at, :])
            if not last:
                whole = ref.from_start[(c + 1) * SPAN - 1 : (c + 1) * SPAN, :]
                new = ref.d_state[...] * whole + new
            ref.d_state[...] = new
        pump(1)
        if c == spans - 1:
            for j in range(PIECES):
                out_sum.across(j)
    d_logs = jnp.concatenate([pair[0] for pair in reversed(d_row)], axis=1)
    d_step = jnp.concatenate([pair[1] for pair in reversed(d_row)], axis=1)
    step = ref.step[...]
    d_dt = (d_step + d_logs * rate) * sigmoid(ref.dt_in[...])
    g_a_log = jnp.sum(d_logs * step, axis=1, keepdims=True) * rate
    g_skip = jnp.sum(jnp.where(ours, ref.sums[1:2, :], 0.0), axis=1, keepdims=True)
    ref.d_dt[...] = d_dt

    small_copies = []
    for place, (h, t) in enumerate(peers):
        theirs = pl.ds(pl.multiple_of((h * tensors + t) * quarter, quarter), quarter)
        small_copies.append(
            send(
                d_bc.at[theirs, :], ref.held_bc.at[place], sem.share, place,
                {"head": h, "tensor": t},
            )
        )
    ref.held_dt[tensor] = ref.d_dt[...]
    for place, t in enumerate(tensor_peers):
        small_copies.append(
            send(ref.d_dt, ref.held_dt.at[tensor], sem.steps, place, {"tensor": t})
        )

    def slope_rows(r):
        at = pl.ds(r, ROWS)
        conv = ref.conv[at, :]
        d_xs = ref.step_wide[at, :] * ref.u[at, :] + skip[...] * ref.d_mixed[at, :]
        ref.d_conv[at, :] = d_xs * silu_slope(conv, sigmoid(conv))

    def unconv_rows(r):
        at = pl.ds(r, ROWS)
        near = ref.d_conv[pl.ds(r, ROWS + 8), :]
        raw = ref.x_pad[pl.ds(r, ROWS + 8), :]
        ref.d_x[at, :] = sum(
            kernel_x[k : k + 1, :] * near[taps - 1 - k : taps - 1 - k + ROWS] for k in range(taps)
        ).astype(LOW)
        for k in range(taps):
            ref.small_mine[k : k + 1, :] += jnp.sum(
                raw[9 - taps + k : 9 - taps + k + ROWS] * near[:ROWS], axis=0, keepdims=True
            )

    ref.small_mine[...] = jnp.zeros((8, I), FULL)
    row_loop(slope_rows)
    row_loop(unconv_rows)
    ref.small_mine[taps : taps + 1, :] = ref.sums[0:1, :]

    def to_others(source, everyone, sems):
        everyone[me] = source[...]
        return [
            send(source, everyone.at[me], sems, k, {"fsdp": other}) for k, other in enumerate(others)
        ]

    def summed(copies, everyone):
        for copy in copies:
            copy.wait_recv()
        value = everyone[0]
        for k in range(1, count):
            value = value + everyone[k]
        return value

    pump(1)
    block.gradient(normed, ref.d_x, ref.g_x)
    scatter_x(0)
    small_all = to_others(ref.small_mine, ref.all_small, sem.small)

    for copy in small_copies:
        copy.wait_recv()
    total_bc = d_bc[mine_at, :].astype(FULL)
    for place in range(size - 1):
        total_bc = total_bc + ref.held_bc[place].astype(FULL)
    total_dt = ref.held_dt[0]
    for t in range(1, tensors):
        total_dt = total_dt + ref.held_dt[t]
    conv = ref.bc_conv[...]
    d_conv = total_bc * silu_slope(conv, sigmoid(conv))
    d_bc_raw = sum(sooner(d_conv, taps - 1 - k) * kernel_bc[:, k : k + 1] for k in range(taps))
    raw = ref.bc_raw[...]
    g_bc = [
        jnp.sum(later(raw, taps - 1 - k) * d_conv, axis=1, keepdims=True) for k in range(taps)
    ]
    blank = jnp.zeros((hc, 1), FULL)
    below = [jnp.sum(total_dt, axis=1, keepdims=True), g_a_log, g_skip] + [blank] * taps
    ref.turn[...] = jnp.zeros((LANES, LANES), FULL)
    for k in range(taps):
        ref.turn[0:quarter, k : k + 1] = g_bc[k]
        ref.turn[quarter : quarter + hc, k : k + 1] = below[k]
    ref.tiny_mine[...] = ref.turn[...].T[0:8]
    tiny_all = to_others(ref.tiny_mine, ref.all_tiny, sem.tiny)
    side_list = [d_bc_raw, total_dt]
    if side_rows > quarter + hc:
        side_list.append(jnp.zeros((side_rows - quarter - hc, T), FULL))
    d_side = jnp.concatenate(side_list, axis=0).astype(LOW)
    s_matrix = block.matrix(ref.all_s)
    if block.turned:
        block.store(ref.g_s, plain(d_side, normed[...]))
    else:
        block.store(ref.g_s, plain(d_side, normed[...]).T)
        s_matrix = s_matrix.astype(FULL).T.astype(LOW)
    scatter_s(0)
    queue += [
        (half_count + step, place, step_at, step)
        for step in range(1, half_count + 1)
        for place, step_at in enumerate((scatter_x, scatter_s))
    ]
    queue.sort(key=lambda entry: entry[:2])
    row = lax.broadcasted_iota(jnp.int32, (side_rows, T), 0)
    once = jnp.where(tensor == 0, quarter + hc, quarter)
    d_side = jnp.where(row < once, d_side.astype(FULL), 0.0).astype(LOW)
    x_matrix = block.matrix(ref.all_x)
    z_matrix = block.matrix(ref.all_z)
    ref.norm_sum[...] = jnp.zeros((8, D), FULL)
    for j in range(PIECES):
        out_sum.close(j)

    def back_piece(h, j):
        at = in_sum.rows(h, j)
        ref.partial_in[at, :] = (
            block.back(ref.d_x[at, :], x_matrix) + block.back(ref.d_z[at, :], z_matrix)
            + ref.side_in[at, :]
        ).astype(LOW)

    ref.side_in[...] = first_axes(d_side, s_matrix)
    for j in range(PIECES):
        for h in head_peers:
            back_piece(h, j)
        in_sum.start(j)
    for j in range(PIECES):
        back_piece(head, j)
        in_sum.across(j)
    pump_until(half_count)
    pump(2)
    for j in range(PIECES):
        in_sum.close(j)
    pump(1)
    ref.norm_mine[...] = ref.norm_sum[...]
    ref.norm_heads[head] = ref.norm_sum[...]
    norm_copies = [
        send(ref.norm_mine, ref.norm_heads.at[head], sem.heads, k, {"head": peer})
        for k, peer in enumerate(head_peers)
    ]
    ref.small[...] = summed(small_all, ref.all_small)
    tiny = summed(tiny_all, ref.all_tiny)
    ref.tiny_sum[...] = tiny
    ref.tiny[group_me] = tiny
    tiny_copies = [
        send(ref.tiny_sum, ref.tiny.at[group_me], sem.gtiny, k, {"head": h, "tensor": t})
        for k, (h, t) in enumerate(peers)
    ]
    for copy in norm_copies:
        copy.wait_recv()
    total = ref.norm_heads[0]
    for k in range(1, heads):
        total = total + ref.norm_heads[k]
    ref.norm_total[...] = total
    norm_all = to_others(ref.norm_total, ref.all_norm, sem.norm)
    pump(2 * count)
    own_bc = ref.own_s[block.slice(0, quarter)]
    ref.own_bc[...] = own_bc if block.turned else ref.own_s[...].T[0:quarter]
    ref.bc_grad[group_me] = ref.own_bc[...]
    own_copies = [
        send(ref.own_bc, ref.bc_grad.at[group_me], sem.gbc, k, {"head": h, "tensor": t})
        for k, (h, t) in enumerate(peers)
    ]
    in_sum.end()
    out_sum.end()
    ref.norm_grad[...] = summed(norm_all, ref.all_norm)
    for copy in tiny_copies + own_copies:
        copy.wait_recv()
    for copy in started:
        copy.wait_send()


def fused(dims, arrays):
    count, heads, tensors = dims["count"], dims["heads"], dims["tensors"]
    taps, state, quarter, side_rows = (dims[k] for k in ("taps", "state", "quarter", "side_rows"))
    block, hw = dims["block"], dims["hw"]
    T, D = arrays["x_in"].shape
    hc = arrays["skip"].shape[1]
    I = hc * hw
    rows, size = D // count, heads * tensors
    spans = T // SPAN
    share = T // heads
    piece = share // PIECES
    wide, low_wide = ((T, I), FULL), ((T, I), LOW)
    shared = lambda columns: ((count,) + block.shape(columns), LOW)
    outs = dict(
        block_out=((T, D), LOW),
        low_in=((T, D), LOW),
        norm_grad=((8, D), FULL),
        own_x=(block.shape(I), FULL),
        own_s=(block.shape(side_rows), FULL),
        own_z=(block.shape(I), FULL),
        own_o=(block.shape(I), FULL),
        small=((8, I), FULL),
        tiny=((size, 8, LANES), FULL),
        bc_grad=((size, quarter, rows), FULL),
    )
    scratch = dict(
        all_x=shared(I),
        g_x=shared(I),
        all_s=shared(side_rows),
        g_s=shared(side_rows),
        all_z=shared(I),
        g_z=shared(I),
        all_o=shared(I),
        g_o=shared(I),
        conv=wide,
        y=wide,
        z=wide,
        gated=wide,
        d_no=wide,
        d_mixed=wide,
        u=wide,
        from_start=wide,
        to_end=wide,
        step_wide=wide,
        act=low_wide,
        v=low_wide,
        v_end=low_wide,
        v_end_low=low_wide,
        normed_out=low_wide,
        d_z=low_wide,
        dy=low_wide,
        dy_start=low_wide,
        dy_start_low=low_wide,
        d_x=low_wide,
        maps=((2 * state, rows), FULL),
        ws=(block.shape(side_rows), LOW),
        kernel_x=((8, I), FULL),
        kernel_all=((2 * state, taps), FULL),
        kernel_bc=((quarter, taps), FULL),
        skip_wide=((1, I), FULL),
        gain=((1, I), FULL),
        x_pad=((T + 8, I), FULL),
        d_conv=((T + 8, I), FULL),
        normed=((T, D), LOW),
        scale_in=((T, 1), FULL),
        columns=((T, LANES), FULL),
        sums=((8, I), FULL),
        bc_raw=((quarter, T), FULL),
        bc_conv=((quarter, T), FULL),
        bc_mine=((quarter, T), LOW),
        bc=((2 * state, T), LOW),
        dt_in=((hc, T), FULL),
        step=((hc, T), FULL),
        cums=((hc, T), FULL),
        cum_columns=((T, hc), FULL),
        running=((state, I), FULL),
        d_state=((state, I), FULL),
        states=((spans, state, I), LOW),
        states_low=((spans, state, I), LOW),
        pair=((8, T), FULL),
        pairs=((size, 8, T), FULL),
        scales=((T, 8), FULL),
        partial_out=((T, D), LOW),
        partial_in=((T, D), LOW),
        side_in=((T, D), FULL),
        d_bc=((2 * state, T), LOW),
        held_bc=((size - 1, quarter, T), LOW),
        d_dt=((hc, T), FULL),
        held_dt=((tensors, hc, T), FULL),
        small_mine=((8, I), FULL),
        all_small=((count, 8, I), FULL),
        turn=((LANES, LANES), FULL),
        tiny_mine=((8, LANES), FULL),
        tiny_sum=((8, LANES), FULL),
        all_tiny=((count, 8, LANES), FULL),
        norm_sum=((8, D), FULL),
        norm_mine=((8, D), FULL),
        norm_total=((8, D), FULL),
        norm_heads=((heads, 8, D), FULL),
        all_norm=((count, 8, D), FULL),
        own_bc=((quarter, rows), FULL),
        out_a=((PIECES, heads - 1, piece, D), LOW),
        out_m=((PIECES, piece, D), LOW),
        out_b=((PIECES, tensors, piece, D), LOW),
        in_a=((PIECES, heads - 1, piece, D), LOW),
        in_m=((PIECES, piece, D), LOW),
        in_b=((PIECES, tensors, piece, D), LOW),
    )
    by_way = lambda columns: [((2, count // 2) + size, LOW) for size in block.sizes(columns)] * 2
    for some in (
        dict(zip(("slot_x0", "slot_x1"), by_way(I))),
        dict(zip(("slot_s0", "slot_s1"), by_way(side_rows))),
        dict(zip(("slot_z0", "slot_z1"), by_way(I))),
        dict(zip(("slot_o0", "slot_o1"), by_way(I))),
    ):
        scratch |= some
    ring = (2, 2, count // 2)
    sems = dict(
        bc=(size - 1,),
        pair=(size - 1,),
        share=(size - 1,),
        steps=(tensors - 1,),
        small=(count - 1,),
        tiny=(count - 1,),
        norm=(count - 1,),
        heads=(heads - 1,),
        gtiny=(size - 1,),
        gbc=(size - 1,),
        gather_x=ring, gather_s=ring, gather_z=ring, gather_o=ring,
        scatter_x=ring, scatter_s=ring, scatter_z=ring, scatter_o=ring,
        out_a=(PIECES, heads - 1),
        out_b=(PIECES, tensors - 1),
        out_c=(PIECES, heads - 1),
        in_a=(PIECES, heads - 1),
        in_b=(PIECES, tensors - 1),
        in_c=(PIECES, heads - 1),
    )
    names = list(arrays) + list(outs) + list(scratch)
    scratch_shapes = [pltpu.VMEM(*shape) for shape in scratch.values()]
    for shape in sems.values():
        scratch_shapes += [pltpu.SemaphoreType.DMA(shape)] * 2
    results = pl.pallas_call(
        partial(block_kernel, dims, names, list(sems)),
        out_shape=[jax.ShapeDtypeStruct(*shape) for shape in outs.values()],
        in_specs=[VMEM_SPEC] * len(arrays),
        out_specs=[VMEM_SPEC] * len(outs),
        scratch_shapes=scratch_shapes,
        compiler_params=pltpu.CompilerParams(
            collective_id=0, has_side_effects=True, vmem_limit_bytes=VMEM_LIMIT
        ),
        name="block",
    )(*arrays.values())
    return SimpleNamespace(**dict(zip(outs, results)))


def finish_kernel(dims, names, passed, results, *args):
    heads, tensors, hw, hc, taps, state, quarter = (
        dims[k] for k in ("heads", "tensors", "hw", "hc", "taps", "state", "quarter")
    )
    given = SimpleNamespace(**dict(zip(names, args)))
    rest = args[len(names) :]
    out = SimpleNamespace(**dict(zip(results, rest)))
    staged, sems = rest[len(results) :]
    T = given.cot.shape[0]
    copies = [
        pltpu.make_async_copy(getattr(given, name), getattr(out, name), sems.at[i])
        for i, name in enumerate(passed)
    ]
    for copy in copies:
        copy.start()
    pieces = 4
    part = T // pieces
    for j in range(pieces):
        at = slice(j * part, (j + 1) * part)

        def grad_rows(i, carry):
            rows = pl.ds(pl.multiple_of(j * part + i * ROWS, ROWS), ROWS)
            staged[rows, :] = given.low_in[rows, :].astype(FULL) + given.cot[
                rows, :
            ].astype(FULL)
            return carry

        lax.fori_loop(0, part // ROWS, grad_rows, 0)
        copy = pltpu.make_async_copy(
            staged.at[at, :], out.grad_in.at[at, :], sems.at[len(passed) + j]
        )
        copy.start()
        copies.append(copy)
    head, tensor = lax.axis_index("head"), lax.axis_index("tensor")
    ours = own_lanes(hc, hw)
    place_of = lane_places(hc, hw)

    def gathered(row):
        return lax.dot_general(
            jnp.where(ours, row, 0.0), place_of, (((1,), (1,)), ((), ())), precision=PRECISE,
            preferred_element_type=FULL,
        )

    out.norm_grad[...] = given.norm_grad[0:1, :]
    maps = jnp.concatenate([given.bc_grad[i] for i in range(heads * tensors)], axis=0).T
    out.w_bc[...] = maps
    turned = dims["block"].turned
    side = given.own_s[...] if turned else given.own_s[...].T
    out.w_dt[...] = side[quarter : quarter + hc]
    for k in range(taps):
        out.conv_x[:, k, :] = gathered(given.small[k : k + 1, :])
    out.gate_gain[...] = gathered(given.small[taps : taps + 1, :])
    tiny = given.tiny
    each = state // quarter
    for i in range(2):
        out.conv_bc[i] = jnp.concatenate(
            [tiny[i * each + j][0:taps, 0:quarter] for j in range(each)], axis=1
        )
    lanes = slice(quarter, quarter + hc)
    out.dt_bias[...] = tiny[head * tensors + tensor][0:1, lanes]
    by_head = tiny[head * tensors]
    for t in range(1, tensors):
        by_head = by_head + tiny[head * tensors + t]
    out.a_log[...] = by_head[1:2, lanes]
    out.skip[...] = by_head[2:3, lanes]
    for copy in copies:
        copy.wait()


def finish(dims, made, cot):
    T, D = cot.shape
    hc, hw, taps, state = (dims[k] for k in ("hc", "hw", "taps", "state"))
    rows = made.bc_grad.shape[2]
    any_spec = pl.BlockSpec(memory_space=pl.ANY)
    large = dict(
        block_out=made.block_out, own_x=made.own_x, own_z=made.own_z, own_o=made.own_o
    )
    shapes = {name: (array.shape, array.dtype) for name, array in large.items()}
    shapes |= dict(grad_in=((T, D), FULL))
    specs = [any_spec] * len(shapes)
    shapes |= dict(
        norm_grad=((1, D), FULL),
        w_bc=((rows, 2 * state), FULL),
        w_dt=((hc, rows), FULL),
        conv_x=((hc, taps, hw), FULL),
        conv_bc=((2, taps, state), FULL),
        dt_bias=((1, hc), FULL),
        a_log=((1, hc), FULL),
        skip=((1, hc), FULL),
        gate_gain=((hc, hw), FULL),
    )
    specs += [VMEM_SPEC] * (len(shapes) - len(specs))
    given = dict(vars(made), cot=cot)
    results = pl.pallas_call(
        partial(finish_kernel, dims, list(given), list(large), list(shapes)),
        out_shape=[jax.ShapeDtypeStruct(*shape) for shape in shapes.values()],
        in_specs=[VMEM_SPEC] * len(given),
        out_specs=specs,
        scratch_shapes=[pltpu.VMEM((T, D), FULL), pltpu.SemaphoreType.DMA((len(large) + 4,))],
        name="finish",
    )(*given.values())
    return SimpleNamespace(**dict(zip(shapes, results)))


def on_device(
    block_in, cotangent, norm_gain, w_x, w_z, w_bc, w_dt, conv_x, conv_bc, dt_bias, a_log, skip,
    gate_gain, w_out,
):
    length, width = block_in.shape
    hc, hw, taps = conv_x.shape
    state = conv_bc.shape[1]
    inner = hc * hw
    heads, tensors, count = (lax.axis_size(a) for a in ("head", "tensor", "fsdp"))
    size = heads * tensors
    quarter = 2 * state // size
    rows = w_x.shape[0]
    block = Block(count, rows)
    used = quarter + hc
    side_rows = used + -used % 16 if block.turned else used + -used % LANES
    assert hw & (hw - 1) == 0 and LANES % hw == 0
    turn = lambda a: a if block.turned else a.T
    arrays = dict(
        x_in=block_in,
        cot=cotangent,
        norm_gain=norm_gain[None, :],
        wx=turn(w_x.transpose(1, 2, 0).reshape(inner, rows)),
        wz=turn(w_z.transpose(1, 2, 0).reshape(inner, rows)),
        wo=turn(w_out.reshape(inner, rows)),
        w_bc=w_bc.reshape(rows, 2 * state),
        w_dt=w_dt.T,
        conv_x=conv_x.transpose(0, 2, 1),
        conv_bc=conv_bc.transpose(0, 2, 1),
        dt_bias=dt_bias[None, :],
        a_log=a_log[None, :],
        skip=skip[None, :],
        gate_gain=gate_gain,
    )
    dims = dict(
        count=count, heads=heads, tensors=tensors, hw=hw, hc=hc, taps=taps, state=state,
        quarter=quarter, block=block, side_rows=side_rows,
    )
    got = finish(dims, fused(dims, arrays), cotangent)
    by_weight = lambda a: turn(a).reshape(hc, hw, rows)
    return (
        got.block_out,
        got.grad_in,
        got.norm_grad.reshape(width),
        by_weight(got.own_x).transpose(2, 0, 1),
        by_weight(got.own_z).transpose(2, 0, 1),
        got.w_bc.reshape(rows, 2, state),
        got.w_dt.T,
        got.conv_x.transpose(0, 2, 1),
        got.conv_bc.transpose(0, 2, 1),
        got.dt_bias.reshape(hc),
        got.a_log.reshape(hc),
        got.skip.reshape(hc),
        got.gate_gain,
        by_weight(got.own_o),
    )


def solution(mesh):
    return jax.shard_map(
        on_device,
        mesh=mesh,
        in_specs=(
            P("fsdp", None),
            P("fsdp", None),
            P(),
            P("fsdp", "head", "tensor"),
            P("fsdp", "head", "tensor"),
            P("fsdp", None, None),
            P("fsdp", "head"),
            P("head", "tensor", None),
            P(),
            P("head"),
            P("head"),
            P("head"),
            P("head", "tensor"),
            P("head", "tensor", "fsdp"),
        ),
        out_specs=(
            P("fsdp", None),
            P("fsdp", None),
            P(),
            P("fsdp", "head", "tensor"),
            P("fsdp", "head", "tensor"),
            P("fsdp", None, None),
            P("fsdp", "head"),
            P("head", "tensor", None),
            P(),
            P("head"),
            P("head"),
            P("head"),
            P("head", "tensor"),
            P("head", "tensor", "fsdp"),
        ),
        check_vma=False,
    )
```

```python
from functools import partial
from types import SimpleNamespace

import jax
import jax.numpy as jnp
from jax import lax
from jax.experimental import pallas as pl
from jax.experimental.pallas import tpu as pltpu
from jax.sharding import PartitionSpec as P

EPSILON = 1e-05
PRECISE = lax.Precision.HIGHEST
LANES = 128
SPAN = 128
ROWS = 32
PIECES = 4
LATE_Z = 2
LATE_OUT = 4
VMEM_LIMIT = 60 * 1024 * 1024
MESH = pl.DeviceIdType.MESH
VMEM_SPEC = pl.BlockSpec(memory_space=pltpu.VMEM)
LOW = jnp.bfloat16
FULL = jnp.float32


def ring_index(position, count):
    high = position // (count // 2)
    return (1 - high) * 2 * position + high * (2 * (count - 1 - position) + 1)


def ring_position(index, count):
    odd = index % 2
    return (1 - odd) * (index // 2) + odd * (count - 1 - index // 2)


def last_axes(a, b):
    return lax.dot_general(a, b, (((1,), (1,)), ((), ())), preferred_element_type=FULL)


def first_axes(a, b):
    return lax.dot_general(a, b, (((0,), (0,)), ((), ())), preferred_element_type=FULL)


def plain(a, b):
    return jnp.dot(a, b, preferred_element_type=FULL)


def high_low(value):
    high = value.astype(LOW)
    return high, (value - high.astype(FULL)).astype(LOW)


def sigmoid(value):
    return 1.0 / (1.0 + jnp.exp(-value))


def silu_slope(value, sigma):
    return sigma * (1.0 + value * (1.0 - sigma))


def softplus(value):
    return jnp.maximum(value, 0.0) + jnp.log1p(jnp.exp(-jnp.abs(value)))


def later(rows, amount):
    if amount == 0:
        return rows
    lane = lax.broadcasted_iota(jnp.int32, rows.shape, 1)
    return jnp.where(lane >= amount, pltpu.roll(rows, amount, 1), 0.0)


def sooner(rows, amount):
    if amount == 0:
        return rows
    length = rows.shape[1]
    lane = lax.broadcasted_iota(jnp.int32, rows.shape, 1)
    return jnp.where(lane < length - amount, pltpu.roll(rows, length - amount, 1), 0.0)


def own_lanes(hc, hw):
    shape = (hc, hc * hw)
    first = lax.broadcasted_iota(jnp.int32, shape, 0) * hw
    lane = lax.broadcasted_iota(jnp.int32, shape, 1)
    return (lane >= first) & (lane < first + hw)


def lane_places(hc, hw):
    shape = (hw, hc * hw)
    lane = lax.broadcasted_iota(jnp.int32, shape, 1)
    place = lax.broadcasted_iota(jnp.int32, shape, 0)
    return jnp.where(jnp.bitwise_and(lane, hw - 1) == place, 1.0, 0.0)


def group_peers(heads, tensors):
    head, tensor = lax.axis_index("head"), lax.axis_index("tensor")
    peers = []
    for offset in range(1, heads * tensors):
        peer_head = (head + offset // tensors) % heads
        peer_tensor = (tensor + offset % tensors) % tensors
        peers.append((peer_head, peer_tensor))
    return head * tensors + tensor, peers


class Block:

    def __init__(self, count, rows):
        self.count, self.rows = count, rows
        self.turned = rows % LANES == 0

    def shape(self, columns):
        return (columns, self.rows) if self.turned else (self.rows, columns)

    def halves(self, ref):
        unit = 16 if self.turned else LANES
        columns = ref.shape[0] if self.turned else ref.shape[1]
        first = (columns // unit + 1) // 2 * unit
        starts = [(0, first), (first, columns - first)] if first < columns else [(0, first)]
        return [self.slice(*start) for start in starts]

    def slice(self, start, amount):
        part = pl.ds(start, amount)
        return (part, slice(None)) if self.turned else (slice(None), part)

    def sizes(self, columns):
        shape = jax.ShapeDtypeStruct(self.shape(columns), LOW)
        return [
            (cut[0].size, self.rows) if self.turned else (self.rows, cut[1].size)
            for cut in self.halves(shape)
        ]

    def matrix(self, ref):
        if self.turned:
            return jnp.concatenate([ref[i] for i in range(self.count)], axis=1)
        return ref[...].reshape(self.count * self.rows, ref.shape[2])

    def project(self, a, matrix):
        return last_axes(a, matrix) if self.turned else plain(a, matrix)

    def back(self, a, matrix):
        return plain(a, matrix) if self.turned else last_axes(a, matrix)

    def store(self, ref, matrix):
        if self.turned:
            for i in range(self.count):
                ref[i] = matrix[:, i * self.rows : (i + 1) * self.rows].astype(ref.dtype)
        else:
            ref[...] = matrix.reshape(ref.shape).astype(ref.dtype)

    def gradient(self, act_ref, d_ref, out_ref):
        if self.turned:
            d = d_ref[...]
            for i in range(self.count):
                part = act_ref[:, i * self.rows : (i + 1) * self.rows]
                out_ref[i] = first_axes(d, part).astype(out_ref.dtype)
        else:
            self.store(out_ref, first_axes(act_ref[...], d_ref[...]))


def block_kernel(dims, given, names, sem_names, *args):
    ref = SimpleNamespace(**dict(zip(names, args)))
    pairs = args[len(names) :]
    sem = SimpleNamespace(
        **{name: (pairs[2 * i], pairs[2 * i + 1]) for i, name in enumerate(sem_names)}
    )
    count, heads, tensors, hw, taps, state, quarter = (
        dims[k] for k in ("count", "heads", "tensors", "hw", "taps", "state", "quarter")
    )
    loads = {
        name: pltpu.make_async_copy(
            getattr(ref, "raw_" + name), getattr(ref, name), args[-1].at[place]
        )
        for place, name in enumerate(given)
    }
    for copy in loads.values():
        copy.start()
    T, D = ref.x_in.shape
    hc = ref.skip.shape[1]
    I = hc * hw
    size = heads * tensors
    block = dims["block"]
    side_rows = dims["side_rows"]
    groups = I // LANES
    per = LANES // hw
    spans = T // SPAN
    head, tensor = lax.axis_index("head"), lax.axis_index("tensor")
    me = lax.axis_index("fsdp")
    group_me, peers = group_peers(heads, tensors)
    position = ring_position(me, count)
    right = ring_index((position + 1) % count, count)
    left = ring_index((position + count - 1) % count, count)
    others = [(me + offset) % count for offset in range(1, count)]
    head_peers = [(head + offset) % heads for offset in range(1, heads)]
    tensor_peers = [(tensor + offset) % tensors for offset in range(1, tensors)]
    started = []

    barrier = pltpu.get_barrier_semaphore()
    for h, t in peers:
        pl.semaphore_signal(barrier, inc=1, device_id={"head": h, "tensor": t}, device_id_type=MESH)
    for other in others:
        pl.semaphore_signal(barrier, inc=1, device_id={"fsdp": other}, device_id_type=MESH)
    pl.semaphore_wait(barrier, len(peers) + len(others))

    def send(source, target, sems, place, device):
        copy = pltpu.make_async_remote_copy(
            src_ref=source,
            dst_ref=target,
            send_sem=sems[0].at[place],
            recv_sem=sems[1].at[place],
            device_id=device,
            device_id_type=MESH,
        )
        copy.start()
        started.append(copy)
        return copy

    half_count = count // 2
    rights = [ring_index((position + count - i) % count, count) for i in range(half_count + 1)]
    lefts = [ring_index((position + i) % count, count) for i in range(half_count + 1)]

    def gather_part(shard, full, sems):
        cuts = block.halves(shard)
        copies = {}

        def step_at(step):
            if step == 0:
                full[me] = shard[...]
            for way, cut in enumerate(cuts):
                for turn, (target, owners) in enumerate(((right, rights), (left, lefts))):
                    if step > 0 and (step < half_count or way == turn):
                        copies[way, turn, step - 1].wait_recv()
                    if step < half_count - 1 or (step == half_count - 1 and way == turn):
                        place = full.at[(owners[step],) + cut]
                        source = shard.at[cut] if step == 0 else place
                        copies[way, turn, step] = send(
                            source, place, sems, (way, turn, step), {"fsdp": target}
                        )

        return step_at

    def scatter_part(grads, own, slots, sems):
        cuts = block.halves(own)
        copies = {}

        def step_at(step):
            for way, cut in enumerate(cuts):
                held = slots[way]
                if step == half_count:
                    total = grads[(me,) + cut].astype(FULL)
                    for turn in range(2):
                        copies[way, turn, step - 1].wait_recv()
                        total = total + held[turn, step - 1].astype(FULL)
                    own[cut] = total
                    continue
                for turn, (target, owners) in enumerate(((right, lefts), (left, rights))):
                    piece = (owners[half_count - step],) + cut
                    if step == 0 and way != turn:
                        continue
                    if step == 0 or (step == 1 and way != turn):
                        source = grads.at[piece]
                    else:
                        copies[way, turn, step - 1].wait_recv()
                        total = held[turn, step - 1].astype(FULL) + grads[piece].astype(FULL)
                        held[turn, step - 1] = total.astype(LOW)
                        source = held.at[turn, step - 1]
                    copies[way, turn, step] = send(
                        source, held.at[turn, step], sems, (way, turn, step), {"fsdp": target}
                    )

        return step_at

    def rounds(parts):
        keyed = [
            (late + step, place, step_at, step)
            for place, (late, step_at) in enumerate(parts)
            for step in range(half_count + 1)
        ]
        keyed.sort(key=lambda entry: entry[:2])
        return keyed

    queue = []

    def pump(amount):
        for _ in range(amount):
            if queue:
                key = queue[0][0]
                while queue and queue[0][0] == key:
                    _, _, step_at, step = queue.pop(0)
                    step_at(step)

    def pump_until(key):
        while queue and queue[0][0] <= key:
            pump(1)

    def row_loop(body, first=0, last=T):
        def run(i, carry):
            body(pl.multiple_of(first + i * ROWS, ROWS))
            return carry

        lax.fori_loop(0, (last - first) // ROWS, run, 0)

    queue += rounds(
        [
            (0, gather_part(ref.wx, ref.all_x, sem.gather_x)),
            (0, lambda step: side_part[0](step)),
            (LATE_Z, gather_part(ref.wz, ref.all_z, sem.gather_z)),
            (LATE_OUT, gather_part(ref.wo, ref.all_o, sem.gather_o)),
        ]
    )
    loads.pop("wx").wait()
    queue.pop(0)[2](0)
    loads.pop("w_bc").wait()
    loads.pop("w_dt").wait()
    maps = ref.w_bc[...].astype(FULL)
    maps = jnp.concatenate([maps[:, i, :] for i in range(2)], axis=1).T
    ref.maps[...] = maps
    mine_at = pl.ds(pl.multiple_of(group_me * quarter, quarter), quarter)
    side_list = [ref.maps[mine_at, :], ref.w_dt[...].astype(FULL)]
    if side_rows > quarter + hc:
        side_list.append(jnp.zeros((side_rows - quarter - hc, maps.shape[1]), FULL))
    side = jnp.concatenate(side_list, axis=0)
    ref.ws[...] = (side if block.turned else side.T).astype(LOW)
    side_part = [gather_part(ref.ws, ref.all_s, sem.gather_s)]
    pump(1)

    def norm_rows(r):
        at = pl.ds(r, ROWS)
        features = ref.x_in[at, :].astype(FULL)
        mean = jnp.mean(features * features, axis=1, keepdims=True)
        scale = lax.rsqrt(mean + EPSILON)
        ref.scale_in[at, :] = scale
        ref.normed[at, :] = (features * scale * ref.norm_gain[...]).astype(LOW)

    for copy in loads.values():
        copy.wait()
    row_loop(norm_rows)
    ref.x_pad[0:8, :] = jnp.zeros((8, I), FULL)
    ref.d_conv[T : T + 8, :] = jnp.zeros((8, I), FULL)
    ref.columns[...] = jnp.zeros((T, LANES), FULL)
    ref.sums[...] = jnp.zeros((8, I), FULL)

    ours = own_lanes(hc, hw)
    place_of = lane_places(hc, hw)
    equal = lax.broadcasted_iota(jnp.int32, (hc, hc), 0) == lax.broadcasted_iota(
        jnp.int32, (hc, hc), 1
    )

    def column(row_ref):
        return jnp.sum(jnp.where(equal, row_ref[...], 0.0), axis=1, keepdims=True)

    def spread(by_head):
        wide = jnp.dot(by_head, place_of, precision=PRECISE, preferred_element_type=FULL)
        return jnp.sum(jnp.where(ours, wide, 0.0), axis=0, keepdims=True)

    for k in range(taps):
        ref.kernel_x[k : k + 1, :] = spread(ref.conv_x[:, k, :])
    ref.gain[...] = spread(ref.gate_gain[...])
    ref.skip_wide[...] = jnp.sum(jnp.where(ours, column(ref.skip), 0.0), axis=0, keepdims=True)
    ref.kernel_all[...] = jnp.concatenate([ref.conv_bc[i].T for i in range(2)], axis=0)
    ref.kernel_bc[...] = ref.kernel_all[mine_at, :]
    expand = jnp.where(ours, 1.0, 0.0).astype(LOW)
    expand_two = jnp.concatenate([expand, expand], axis=0)

    def widen(rows):
        return first_axes(jnp.concatenate(high_low(rows), axis=0), expand_two)

    def narrow(wide):
        high, low = high_low(wide)
        return last_axes(expand, high) + last_axes(expand, low)

    pump_until(half_count)

    normed = ref.normed
    if block.turned:
        side = last_axes(block.matrix(ref.all_s), normed[...])
    else:
        side = plain(normed[...], block.matrix(ref.all_s)).T
    bc_raw = side[0:quarter]
    ref.bc_raw[...] = bc_raw
    kernel_bc = ref.kernel_bc
    bc_conv = sum(later(bc_raw, taps - 1 - k) * kernel_bc[:, k : k + 1] for k in range(taps))
    ref.bc_conv[...] = bc_conv
    ref.bc_mine[...] = (bc_conv * sigmoid(bc_conv)).astype(LOW)
    bc = ref.bc
    bc_copies = [
        send(ref.bc_mine, bc.at[mine_at, :], sem.bc, place, {"head": h, "tensor": t})
        for place, (h, t) in enumerate(peers)
    ]
    bc[mine_at, :] = ref.bc_mine[...]

    half = T // 2
    x_matrix = block.matrix(ref.all_x)
    for first in (0, half):
        ref.x_pad[8 + first : 8 + first + half, :] = block.project(
            normed[first : first + half, :], x_matrix
        )

    dt_in = side[quarter : quarter + hc] + column(ref.dt_bias)
    step = softplus(dt_in)
    rate = -jnp.exp(column(ref.a_log))
    logs = step * rate
    ref.dt_in[...] = dt_in
    ref.step[...] = step
    sooner_row = lax.broadcasted_iota(jnp.int32, (SPAN, SPAN), 0)
    later_lane = lax.broadcasted_iota(jnp.int32, (SPAN, SPAN), 1)
    upper = jnp.where(sooner_row <= later_lane, 1.0, 0.0)
    lower = jnp.where(sooner_row >= later_lane, 1.0, 0.0)
    causal = sooner_row >= later_lane
    cums, to_end = [], []
    for c in range(spans):
        part = jnp.dot(
            logs[:, c * SPAN : (c + 1) * SPAN], upper, precision=PRECISE, preferred_element_type=FULL
        )
        cums.append(part)
        to_end.append(part[:, SPAN - 1 : SPAN] - part)
    cums = jnp.concatenate(cums, axis=1)
    ref.cums[...] = cums
    ref.cum_columns[...] = cums.T
    ref.from_start[...] = widen(jnp.exp(cums))
    ref.to_end[...] = widen(jnp.exp(jnp.concatenate(to_end, axis=1)))
    ref.step_wide[...] = widen(step)

    kernel_x = ref.kernel_x

    def conv_rows(r):
        at = pl.ds(r, ROWS)
        near = ref.x_pad[pl.ds(r, ROWS + 8), :]
        conv = sum(
            kernel_x[k : k + 1, :] * near[9 - taps + k : 9 - taps + k + ROWS] for k in range(taps)
        )
        ref.conv[at, :] = conv
        act = (conv * sigmoid(conv)).astype(LOW)
        ref.act[at, :] = act
        v = act.astype(FULL) * ref.step_wide[at, :]
        ref.v[at, :] = v.astype(LOW)
        ref.v_end[at, :], ref.v_end_low[at, :] = high_low(v * ref.to_end[at, :])

    row_loop(conv_rows)
    pump(1)
    for copy in bc_copies:
        copy.wait_recv()

    head_lane = lax.broadcasted_iota(jnp.int32, (SPAN, LANES), 1)
    lanes_of = [(head_lane >= i * hw) & (head_lane < (i + 1) * hw) for i in range(per)]

    def maps_of(c):
        at = slice(c * SPAN, (c + 1) * SPAN)
        return bc[0:state, at], bc[state : 2 * state, at]

    def decay_of(c, h):
        at = slice(c * SPAN, (c + 1) * SPAN)
        gap = ref.cum_columns[at, h : h + 1] - ref.cums[h : h + 1, at]
        return jnp.exp(jnp.where(causal, gap, -1e30))

    y = ref.y
    for c in range(spans):
        at = slice(c * SPAN, (c + 1) * SPAN)
        b_map, c_map = maps_of(c)
        scores = first_axes(c_map, b_map)
        if c > 0:
            y[at, :] = (first_axes(c_map, ref.states[c]) + first_axes(c_map, ref.states_low[c])) * ref.from_start[at, :]
        for g in range(groups):
            lanes = slice(g * LANES, (g + 1) * LANES)
            v = ref.v[at, lanes]
            weights, values = [], []
            for i in range(per):
                weights.append((scores * decay_of(c, g * per + i)).astype(LOW))
                values.append(jnp.where(lanes_of[i], v, jnp.zeros_like(v)))
            part = plain(jnp.concatenate(weights, axis=1), jnp.concatenate(values, axis=0))
            y[at, lanes] = part if c == 0 else y[at, lanes] + part
        if c + 1 < spans:
            new = plain(b_map, ref.v_end[at, :]) + plain(b_map, ref.v_end_low[at, :])
            if c > 0:
                whole = ref.from_start[(c + 1) * SPAN - 1 : (c + 1) * SPAN, :]
                new = ref.running[...] * whole + new
            ref.running[...] = new
            ref.states[c + 1], ref.states_low[c + 1] = high_low(new)

    pump_until(LATE_Z + half_count)
    z_matrix = block.matrix(ref.all_z)
    for first in (0, half):
        ref.z[first : first + half, :] = block.project(normed[first : first + half, :], z_matrix)
    skip = ref.skip_wide
    gain = ref.gain
    columns = ref.columns

    def gate_rows(r):
        at = pl.ds(r, ROWS)
        z = ref.z[at, :]
        mixed = y[at, :] + skip[...] * ref.act[at, :].astype(FULL)
        gated = mixed * (z * sigmoid(z))
        ref.gated[at, :] = gated
        columns[at, 0:1] = jnp.sum(gated * gated, axis=1, keepdims=True)

    row_loop(gate_rows)

    def exchanged(lane, mine, everyone, sems):
        mine[...] = columns[...].T[lane : lane + 1]
        everyone[group_me] = mine[...]
        copies = [
            send(mine, everyone.at[group_me], sems, place, {"head": h, "tensor": t})
            for place, (h, t) in enumerate(peers)
        ]
        pump(1)
        for copy in copies:
            copy.wait_recv()
        total = everyone[0]
        for k in range(1, size):
            total = total + everyone[k]
        return total

    full_inner = I * size
    squares = exchanged(0, ref.square, ref.squares, sem.square)
    scale_row = lax.rsqrt(squares / full_inner + EPSILON)
    ref.scale_row[...] = scale_row
    ref.scales[...] = jnp.concatenate([scale_row, jnp.zeros((7, T), FULL)], axis=0).T

    def normed_out_rows(r):
        at = pl.ds(r, ROWS)
        hat = ref.gated[at, :] * ref.scales[at, 0:1]
        ref.normed_out[at, :] = (hat * gain[...]).astype(LOW)

    row_loop(normed_out_rows)
    block.gradient(ref.cot, ref.normed_out, ref.g_o)
    scatter_o = scatter_part(ref.g_o, ref.own_o, (ref.slot_o0, ref.slot_o1), sem.scatter_o)
    scatter_z = scatter_part(ref.g_z, ref.own_z, (ref.slot_z0, ref.slot_z1), sem.scatter_z)
    scatter_x = scatter_part(ref.g_x, ref.own_x, (ref.slot_x0, ref.slot_x1), sem.scatter_x)
    scatter_s = scatter_part(ref.g_s, ref.own_s, (ref.slot_s0, ref.slot_s1), sem.scatter_s)
    last_key = LATE_OUT + half_count

    def enqueue(parts, key):
        for place, step_at in enumerate(parts):
            queue.extend((key + step, place, step_at, step) for step in range(1, half_count + 1))
        queue.sort(key=lambda entry: entry[:2])

    scatter_o(0)
    enqueue([scatter_o], last_key - 1.5)
    pump_until(last_key)

    o_matrix = block.matrix(ref.all_o)
    for first in (0, half):
        ref.d_no[first : first + half, :] = block.project(
            ref.cot[first : first + half, :], o_matrix
        )

    def inner_rows(r):
        at = pl.ds(r, ROWS)
        columns[at, 1:2] = jnp.sum(
            ref.d_no[at, :] * gain[...] * ref.gated[at, :], axis=1, keepdims=True
        )

    row_loop(inner_rows)
    inner_sum = exchanged(1, ref.product, ref.products, sem.product)
    scale_row = ref.scale_row[...]
    third_row = scale_row * scale_row * scale_row * (inner_sum / full_inner)
    ref.thirds[...] = jnp.concatenate([third_row, jnp.zeros((7, T), FULL)], axis=0).T

    def gate_back_rows(r):
        at = pl.ds(r, ROWS)
        scale = ref.scales[at, 0:1]
        third = ref.thirds[at, 0:1]
        gated, d_no, z = ref.gated[at, :], ref.d_no[at, :], ref.z[at, :]
        act = ref.act[at, :].astype(FULL)
        hat = gated * scale
        d_gated = scale * (d_no * gain[...]) - gated * third
        sigma = sigmoid(z)
        d_mixed = d_gated * (z * sigma)
        mixed = y[at, :] + skip[...] * act
        ref.d_z[at, :] = (d_gated * mixed * silu_slope(z, sigma)).astype(LOW)
        ref.d_mixed[at, :] = d_mixed
        ref.dy[at, :] = d_mixed.astype(LOW)
        ref.dy_start[at, :], ref.dy_start_low[at, :] = high_low(d_mixed * ref.from_start[at, :])
        ref.sums[0:1, :] += jnp.sum(d_no * hat, axis=0, keepdims=True)
        ref.sums[1:2, :] += jnp.sum(d_mixed * act, axis=0, keepdims=True)

    row_loop(gate_back_rows)

    pump(1)
    block.gradient(normed, ref.d_z, ref.g_z)
    scatter_z(0)
    enqueue([scatter_z], last_key + 1.2)

    share = T // heads
    piece = share // PIECES

    class GroupSum:
        def __init__(self, source, result, finish, held, sems):
            self.source, self.result, self.finish = source, result, finish
            self.by_head, self.middle, self.by_tensor = held
            self.sems = sems
            self.from_head, self.from_tensor, self.back = {}, {}, {}

        def rows(self, h, j):
            return pl.ds(pl.multiple_of(h * share + j * piece, piece), piece)

        def start(self, j):
            self.from_head[j] = [
                send(
                    self.source.at[self.rows(peer, j), :], self.by_head.at[j, k], self.sems[0],
                    (j, k), {"head": peer},
                )
                for k, peer in enumerate(head_peers)
            ]

        def across(self, j):
            for copy in self.from_head[j]:
                copy.wait_recv()
            total = self.source[self.rows(head, j), :].astype(FULL)
            for k in range(heads - 1):
                total = total + self.by_head[j, k].astype(FULL)
            total = total.astype(LOW)
            self.middle[j] = total
            self.by_tensor[j, tensor] = total
            self.from_tensor[j] = [
                send(
                    self.middle.at[j], self.by_tensor.at[j, tensor], self.sems[1], (j, k),
                    {"tensor": peer},
                )
                for k, peer in enumerate(tensor_peers)
            ]

        def close(self, j):
            for copy in self.from_tensor[j]:
                copy.wait_recv()
            total = self.by_tensor[j, 0].astype(FULL)
            for k in range(1, tensors):
                total = total + self.by_tensor[j, k].astype(FULL)
            at = self.rows(head, j)
            self.result[at, :] = self.finish(at, total).astype(LOW)
            self.back[j] = [
                send(
                    self.result.at[at, :], self.result.at[at, :], self.sems[2], (j, k),
                    {"head": peer},
                )
                for k, peer in enumerate(head_peers)
            ]

        def end(self):
            for j in range(PIECES):
                for copy in self.back[j]:
                    copy.wait_recv()

    def finish_out(at, total):
        return total + ref.x_in[at, :].astype(FULL)

    norm_gain = ref.norm_gain

    def finish_in(at, total):
        features = ref.x_in[at, :].astype(FULL)
        scale = ref.scale_in[at, :]
        ref.norm_sum[0:1, :] += jnp.sum(total * (features * scale), axis=0, keepdims=True)
        inner = total * norm_gain[...]
        mean = jnp.mean(inner * features, axis=1, keepdims=True)
        return scale * inner - features * (scale * scale * scale * mean)

    out_sum = GroupSum(
        ref.partial_out, ref.block_out, finish_out, (ref.out_a, ref.out_m, ref.out_b),
        (sem.out_a, sem.out_b, sem.out_c),
    )
    in_sum = GroupSum(
        ref.partial_in, ref.low_in, finish_in, (ref.in_a, ref.in_m, ref.in_b),
        (sem.in_a, sem.in_b, sem.in_c),
    )
    for first in (0, half):
        ref.partial_out[first : first + half, :] = block.back(
            ref.normed_out[first : first + half, :], o_matrix
        ).astype(LOW)
    for j in range(PIECES):
        out_sum.start(j)

    d_bc = ref.d_bc
    d_row = []
    for c in reversed(range(spans)):
        at = slice(c * SPAN, (c + 1) * SPAN)
        b_map, c_map = maps_of(c)
        scores = first_axes(c_map, b_map)
        d_scores = jnp.zeros((SPAN, SPAN), FULL)
        last = c + 1 == spans
        if not last:
            low_d_state, lower_d_state = high_low(ref.d_state[...])
            ref.u[at, :] = (first_axes(b_map, low_d_state) + first_axes(b_map, lower_d_state)) * ref.to_end[at, :]
        for g in range(groups):
            lanes = slice(g * LANES, (g + 1) * LANES)
            v = ref.v[at, lanes]
            dy = ref.dy[at, lanes]
            dy_turned = dy.astype(FULL).T.astype(LOW)
            lane_row = lax.broadcasted_iota(jnp.int32, (LANES, SPAN), 0)
            weights, values = [], []
            for i in range(per):
                decay = decay_of(c, g * per + i)
                weights.append((scores * decay).astype(LOW))
                mine = (lane_row >= i * hw) & (lane_row < (i + 1) * hw)
                values.append(jnp.where(mine, dy_turned, jnp.zeros_like(dy_turned)))
                own_dy = jnp.where(lanes_of[i], dy, jnp.zeros_like(dy))
                d_scores = d_scores + last_axes(own_dy, v) * decay
            part = plain(jnp.concatenate(values, axis=1), jnp.concatenate(weights, axis=0)).T
            ref.u[at, lanes] = part if last else ref.u[at, lanes] + part
        low_d = d_scores.astype(LOW)
        d_b = plain(c_map, low_d)
        d_c = last_axes(b_map, low_d)
        if not last:
            d_b = d_b + last_axes(low_d_state, ref.v_end[at, :])
        if c > 0:
            d_c = d_c + last_axes(ref.states[c], ref.dy_start[at, :])
        d_bc[0:state, at] = d_b.astype(LOW)
        d_bc[state : 2 * state, at] = d_c.astype(LOW)

        u = ref.u[at, :]
        balance = narrow(
            ref.dy[at, :].astype(FULL) * y[at, :] - ref.v[at, :].astype(FULL) * u
        )
        d_logs = jnp.dot(balance, lower, precision=PRECISE, preferred_element_type=FULL)
        if not last:
            passed = jnp.sum(
                (ref.states[c + 1].astype(FULL) + ref.states_low[c + 1].astype(FULL)) * ref.d_state[...], axis=0, keepdims=True
            )
            passed = jnp.sum(jnp.where(ours, passed, 0.0), axis=1, keepdims=True)
            d_logs = d_logs + passed
        d_step = narrow(ref.act[at, :].astype(FULL) * u)
        d_row.append((d_logs, d_step))
        if c > 0:
            new = plain(c_map, ref.dy_start[at, :]) + plain(c_map, ref.dy_start_low[at, :])
            if not last:
                whole = ref.from_start[(c + 1) * SPAN - 1 : (c + 1) * SPAN, :]
                new = ref.d_state[...] * whole + new
            ref.d_state[...] = new
        if c == spans - 1:
            for j in range(PIECES):
                out_sum.across(j)
        if c % 2:
            pump(1)
    d_logs = jnp.concatenate([pair[0] for pair in reversed(d_row)], axis=1)
    d_step = jnp.concatenate([pair[1] for pair in reversed(d_row)], axis=1)
    step = ref.step[...]
    d_dt = (d_step + d_logs * rate) * sigmoid(ref.dt_in[...])
    g_a_log = jnp.sum(d_logs * step, axis=1, keepdims=True) * rate
    g_skip = jnp.sum(jnp.where(ours, ref.sums[1:2, :], 0.0), axis=1, keepdims=True)
    ref.d_dt[...] = d_dt

    small_copies = []
    for place, (h, t) in enumerate(peers):
        theirs = pl.ds(pl.multiple_of((h * tensors + t) * quarter, quarter), quarter)
        small_copies.append(
            send(
                d_bc.at[theirs, :], ref.held_bc.at[place], sem.share, place,
                {"head": h, "tensor": t},
            )
        )
    ref.held_dt[tensor] = ref.d_dt[...]
    for place, t in enumerate(tensor_peers):
        small_copies.append(
            send(ref.d_dt, ref.held_dt.at[tensor], sem.steps, place, {"tensor": t})
        )

    def slope_rows(r):
        at = pl.ds(r, ROWS)
        conv = ref.conv[at, :]
        d_xs = ref.step_wide[at, :] * ref.u[at, :] + skip[...] * ref.d_mixed[at, :]
        ref.d_conv[at, :] = d_xs * silu_slope(conv, sigmoid(conv))

    def unconv_rows(r):
        at = pl.ds(r, ROWS)
        near = ref.d_conv[pl.ds(r, ROWS + 8), :]
        raw = ref.x_pad[pl.ds(r, ROWS + 8), :]
        ref.d_x[at, :] = sum(
            kernel_x[k : k + 1, :] * near[taps - 1 - k : taps - 1 - k + ROWS] for k in range(taps)
        ).astype(LOW)
        for k in range(taps):
            ref.small_mine[k : k + 1, :] += jnp.sum(
                raw[9 - taps + k : 9 - taps + k + ROWS] * near[:ROWS], axis=0, keepdims=True
            )

    ref.small_mine[...] = jnp.zeros((8, I), FULL)
    row_loop(slope_rows)
    row_loop(unconv_rows)
    ref.small_mine[taps : taps + 1, :] = ref.sums[0:1, :]

    def to_others(source, everyone, sems):
        everyone[me] = source[...]
        return [
            send(source, everyone.at[me], sems, k, {"fsdp": other}) for k, other in enumerate(others)
        ]

    def summed(copies, everyone):
        for copy in copies:
            copy.wait_recv()
        value = everyone[0]
        for k in range(1, count):
            value = value + everyone[k]
        return value

    block.gradient(normed, ref.d_x, ref.g_x)
    scatter_x(0)
    pump(1)
    small_all = to_others(ref.small_mine, ref.all_small, sem.small)

    for copy in small_copies:
        copy.wait_recv()
    total_bc = d_bc[mine_at, :].astype(FULL)
    for place in range(size - 1):
        total_bc = total_bc + ref.held_bc[place].astype(FULL)
    total_dt = ref.held_dt[0]
    for t in range(1, tensors):
        total_dt = total_dt + ref.held_dt[t]
    conv = ref.bc_conv[...]
    d_conv = total_bc * silu_slope(conv, sigmoid(conv))
    d_bc_raw = sum(sooner(d_conv, taps - 1 - k) * kernel_bc[:, k : k + 1] for k in range(taps))
    raw = ref.bc_raw[...]
    g_bc = [
        jnp.sum(later(raw, taps - 1 - k) * d_conv, axis=1, keepdims=True) for k in range(taps)
    ]
    blank = jnp.zeros((hc, 1), FULL)
    below = [jnp.sum(total_dt, axis=1, keepdims=True), g_a_log, g_skip] + [blank] * taps
    ref.turn[...] = jnp.zeros((LANES, LANES), FULL)
    for k in range(taps):
        ref.turn[0:quarter, k : k + 1] = g_bc[k]
        ref.turn[quarter : quarter + hc, k : k + 1] = below[k]
    ref.tiny_mine[...] = ref.turn[...].T[0:8]
    tiny_all = to_others(ref.tiny_mine, ref.all_tiny, sem.tiny)
    side_list = [d_bc_raw, total_dt]
    if side_rows > quarter + hc:
        side_list.append(jnp.zeros((side_rows - quarter - hc, T), FULL))
    d_side = jnp.concatenate(side_list, axis=0).astype(LOW)
    s_matrix = block.matrix(ref.all_s)
    if block.turned:
        block.store(ref.g_s, plain(d_side, normed[...]))
    else:
        block.store(ref.g_s, plain(d_side, normed[...]).T)
        s_matrix = s_matrix.astype(FULL).T.astype(LOW)
    scatter_s(0)
    enqueue([scatter_x, scatter_s], last_key + 4.6)
    row = lax.broadcasted_iota(jnp.int32, (side_rows, T), 0)
    once = jnp.where(tensor == 0, quarter + hc, quarter)
    d_side = jnp.where(row < once, d_side.astype(FULL), 0.0).astype(LOW)
    x_matrix = block.matrix(ref.all_x)
    z_matrix = block.matrix(ref.all_z)
    ref.norm_sum[...] = jnp.zeros((1, D), FULL)
    for j in range(PIECES):
        out_sum.close(j)

    def back_piece(h, j):
        at = in_sum.rows(h, j)
        ref.partial_in[at, :] = (
            block.back(ref.d_x[at, :], x_matrix) + block.back(ref.d_z[at, :], z_matrix)
            + ref.side_in[at, :]
        ).astype(LOW)

    ref.side_in[...] = first_axes(d_side, s_matrix)
    for j in range(PIECES):
        for h in head_peers:
            back_piece(h, j)
        in_sum.start(j)
    pump(1)
    for j in range(PIECES):
        back_piece(head, j)
        in_sum.across(j)
    for j in range(PIECES):
        pump(1)
        in_sum.close(j)
    ref.norm_mine[...] = ref.norm_sum[...]
    ref.norm_heads[head] = ref.norm_sum[...]
    norm_copies = [
        send(ref.norm_mine, ref.norm_heads.at[head], sem.heads, k, {"head": peer})
        for k, peer in enumerate(head_peers)
    ]
    ref.small[...] = summed(small_all, ref.all_small)
    tiny = summed(tiny_all, ref.all_tiny)
    ref.tiny_sum[...] = tiny
    ref.tiny[group_me] = tiny
    tiny_copies = [
        send(ref.tiny_sum, ref.tiny.at[group_me], sem.gtiny, k, {"head": h, "tensor": t})
        for k, (h, t) in enumerate(peers)
    ]
    for copy in norm_copies:
        copy.wait_recv()
    total = ref.norm_heads[0]
    for k in range(1, heads):
        total = total + ref.norm_heads[k]
    ref.norm_total[...] = total
    norm_all = to_others(ref.norm_total, ref.all_norm, sem.norm)
    pump(4 * count)
    own_bc = ref.own_s[block.slice(0, quarter)]
    ref.own_bc[...] = own_bc if block.turned else ref.own_s[...].T[0:quarter]
    ref.bc_grad[group_me] = ref.own_bc[...]
    own_copies = [
        send(ref.own_bc, ref.bc_grad.at[group_me], sem.gbc, k, {"head": h, "tensor": t})
        for k, (h, t) in enumerate(peers)
    ]
    in_sum.end()
    out_sum.end()
    ref.norm_grad[...] = summed(norm_all, ref.all_norm)
    for copy in tiny_copies + own_copies:
        copy.wait_recv()
    for copy in started:
        copy.wait_send()


def fused(dims, arrays):
    count, heads, tensors = dims["count"], dims["heads"], dims["tensors"]
    taps, state, quarter, side_rows = (dims[k] for k in ("taps", "state", "quarter", "side_rows"))
    block, hw = dims["block"], dims["hw"]
    T, D = arrays["x_in"].shape
    hc = arrays["skip"].shape[1]
    I = hc * hw
    rows, size = D // count, heads * tensors
    spans = T // SPAN
    share = T // heads
    piece = share // PIECES
    wide, low_wide = ((T, I), FULL), ((T, I), LOW)
    shared = lambda columns: ((count,) + block.shape(columns), LOW)
    outs = dict(
        block_out=((T, D), LOW),
        low_in=((T, D), LOW),
        norm_grad=((1, D), FULL),
        own_x=(block.shape(I), FULL),
        own_s=(block.shape(side_rows), FULL),
        own_z=(block.shape(I), FULL),
        own_o=(block.shape(I), FULL),
        small=((8, I), FULL),
        tiny=((size, 8, LANES), FULL),
        bc_grad=((size, quarter, rows), FULL),
    )
    scratch = dict(
        all_x=shared(I),
        g_x=shared(I),
        all_s=shared(side_rows),
        g_s=shared(side_rows),
        all_z=shared(I),
        g_z=shared(I),
        all_o=shared(I),
        g_o=shared(I),
        conv=wide,
        y=wide,
        z=wide,
        gated=wide,
        d_no=wide,
        d_mixed=wide,
        u=wide,
        from_start=wide,
        to_end=wide,
        step_wide=wide,
        act=low_wide,
        v=low_wide,
        v_end=low_wide,
        v_end_low=low_wide,
        normed_out=low_wide,
        d_z=low_wide,
        dy=low_wide,
        dy_start=low_wide,
        dy_start_low=low_wide,
        d_x=low_wide,
        maps=((2 * state, rows), FULL),
        ws=(block.shape(side_rows), LOW),
        kernel_x=((8, I), FULL),
        kernel_all=((2 * state, taps), FULL),
        kernel_bc=((quarter, taps), FULL),
        skip_wide=((1, I), FULL),
        gain=((1, I), FULL),
        x_pad=((T + 8, I), FULL),
        d_conv=((T + 8, I), FULL),
        normed=((T, D), LOW),
        scale_in=((T, 1), FULL),
        columns=((T, LANES), FULL),
        sums=((8, I), FULL),
        bc_raw=((quarter, T), FULL),
        bc_conv=((quarter, T), FULL),
        bc_mine=((quarter, T), LOW),
        bc=((2 * state, T), LOW),
        dt_in=((hc, T), FULL),
        step=((hc, T), FULL),
        cums=((hc, T), FULL),
        cum_columns=((T, hc), FULL),
        running=((state, I), FULL),
        d_state=((state, I), FULL),
        states=((spans, state, I), LOW),
        states_low=((spans, state, I), LOW),
        square=((1, T), FULL),
        squares=((size, 1, T), FULL),
        product=((1, T), FULL),
        products=((size, 1, T), FULL),
        scale_row=((1, T), FULL),
        thirds=((T, 8), FULL),
        scales=((T, 8), FULL),
        partial_out=((T, D), LOW),
        partial_in=((T, D), LOW),
        side_in=((T, D), FULL),
        d_bc=((2 * state, T), LOW),
        held_bc=((size - 1, quarter, T), LOW),
        d_dt=((hc, T), FULL),
        held_dt=((tensors, hc, T), FULL),
        small_mine=((8, I), FULL),
        all_small=((count, 8, I), FULL),
        turn=((LANES, LANES), FULL),
        tiny_mine=((8, LANES), FULL),
        tiny_sum=((8, LANES), FULL),
        all_tiny=((count, 8, LANES), FULL),
        norm_sum=((1, D), FULL),
        norm_mine=((1, D), FULL),
        norm_total=((1, D), FULL),
        norm_heads=((heads, 1, D), FULL),
        all_norm=((count, 1, D), FULL),
        own_bc=((quarter, rows), FULL),
        out_a=((PIECES, heads - 1, piece, D), LOW),
        out_m=((PIECES, piece, D), LOW),
        out_b=((PIECES, tensors, piece, D), LOW),
        in_a=((PIECES, heads - 1, piece, D), LOW),
        in_m=((PIECES, piece, D), LOW),
        in_b=((PIECES, tensors, piece, D), LOW),
    )
    by_way = lambda columns: [((2, count // 2) + size, LOW) for size in block.sizes(columns)] * 2
    for some in (
        dict(zip(("slot_x0", "slot_x1"), by_way(I))),
        dict(zip(("slot_s0", "slot_s1"), by_way(side_rows))),
        dict(zip(("slot_z0", "slot_z1"), by_way(I))),
        dict(zip(("slot_o0", "slot_o1"), by_way(I))),
    ):
        scratch |= some
    ring = (2, 2, count // 2)
    sems = dict(
        bc=(size - 1,),
        square=(size - 1,),
        product=(size - 1,),
        share=(size - 1,),
        steps=(tensors - 1,),
        small=(count - 1,),
        tiny=(count - 1,),
        norm=(count - 1,),
        heads=(heads - 1,),
        gtiny=(size - 1,),
        gbc=(size - 1,),
        gather_x=ring, gather_s=ring, gather_z=ring, gather_o=ring,
        scatter_x=ring, scatter_s=ring, scatter_z=ring, scatter_o=ring,
        out_a=(PIECES, heads - 1),
        out_b=(PIECES, tensors - 1),
        out_c=(PIECES, heads - 1),
        in_a=(PIECES, heads - 1),
        in_b=(PIECES, tensors - 1),
        in_c=(PIECES, heads - 1),
    )
    scratch |= {name: (array.shape, array.dtype) for name, array in arrays.items()}
    names = ["raw_" + name for name in arrays] + list(outs) + list(scratch)
    scratch_shapes = [pltpu.VMEM(*shape) for shape in scratch.values()]
    for shape in sems.values():
        scratch_shapes += [pltpu.SemaphoreType.DMA(shape)] * 2
    scratch_shapes.append(pltpu.SemaphoreType.DMA((len(arrays),)))
    results = pl.pallas_call(
        partial(block_kernel, dims, list(arrays), names, list(sems)),
        out_shape=[jax.ShapeDtypeStruct(*shape) for shape in outs.values()],
        in_specs=[pl.BlockSpec(memory_space=pltpu.HBM)] * len(arrays),
        out_specs=[VMEM_SPEC] * len(outs),
        scratch_shapes=scratch_shapes,
        compiler_params=pltpu.CompilerParams(
            collective_id=0, has_side_effects=True, vmem_limit_bytes=VMEM_LIMIT
        ),
        name="block",
    )(*arrays.values())
    return SimpleNamespace(**dict(zip(outs, results)))


def finish_kernel(dims, names, passed, results, *args):
    heads, tensors, hw, hc, taps, state, quarter = (
        dims[k] for k in ("heads", "tensors", "hw", "hc", "taps", "state", "quarter")
    )
    given = SimpleNamespace(**dict(zip(names, args)))
    rest = args[len(names) :]
    out = SimpleNamespace(**dict(zip(results, rest)))
    staged, sems = rest[len(results) :]
    T = given.cot.shape[0]
    copies = [
        pltpu.make_async_copy(getattr(given, name), getattr(out, name), sems.at[i])
        for i, name in enumerate(passed)
    ]
    for copy in copies:
        copy.start()
    pieces = 4
    part = T // pieces
    for j in range(pieces):
        at = slice(j * part, (j + 1) * part)

        def grad_rows(i, carry):
            rows = pl.ds(pl.multiple_of(j * part + i * ROWS, ROWS), ROWS)
            staged[rows, :] = given.low_in[rows, :].astype(FULL) + given.cot[
                rows, :
            ].astype(FULL)
            return carry

        lax.fori_loop(0, part // ROWS, grad_rows, 0)
        copy = pltpu.make_async_copy(
            staged.at[at, :], out.grad_in.at[at, :], sems.at[len(passed) + j]
        )
        copy.start()
        copies.append(copy)
    head, tensor = lax.axis_index("head"), lax.axis_index("tensor")
    ours = own_lanes(hc, hw)
    place_of = lane_places(hc, hw)

    def gathered(row):
        return lax.dot_general(
            jnp.where(ours, row, 0.0), place_of, (((1,), (1,)), ((), ())), precision=PRECISE,
            preferred_element_type=FULL,
        )

    out.norm_grad[...] = given.norm_grad[0:1, :]
    maps = jnp.concatenate([given.bc_grad[i] for i in range(heads * tensors)], axis=0).T
    for i in range(2):
        out.w_bc[:, i, :] = maps[:, i * state : (i + 1) * state]
    turned = dims["block"].turned
    side = given.own_s[...] if turned else given.own_s[...].T
    out.w_dt[...] = side[quarter : quarter + hc]
    for k in range(taps):
        out.conv_x[:, k, :] = gathered(given.small[k : k + 1, :])
    out.gate_gain[...] = gathered(given.small[taps : taps + 1, :])
    tiny = given.tiny
    each = state // quarter
    for i in range(2):
        out.conv_bc[i] = jnp.concatenate(
            [tiny[i * each + j][0:taps, 0:quarter] for j in range(each)], axis=1
        )
    lanes = slice(quarter, quarter + hc)
    out.dt_bias[...] = tiny[head * tensors + tensor][0:1, lanes]
    by_head = tiny[head * tensors]
    for t in range(1, tensors):
        by_head = by_head + tiny[head * tensors + t]
    out.a_log[...] = by_head[1:2, lanes]
    out.skip[...] = by_head[2:3, lanes]
    for copy in copies:
        copy.wait()


def finish(dims, made, cot):
    T, D = cot.shape
    hc, hw, taps, state = (dims[k] for k in ("hc", "hw", "taps", "state"))
    rows = made.bc_grad.shape[2]
    any_spec = pl.BlockSpec(memory_space=pl.ANY)
    large = dict(
        block_out=made.block_out, own_x=made.own_x, own_z=made.own_z, own_o=made.own_o
    )
    shapes = {name: (array.shape, array.dtype) for name, array in large.items()}
    shapes |= dict(grad_in=((T, D), FULL))
    specs = [any_spec] * len(shapes)
    shapes |= dict(
        norm_grad=((1, D), FULL),
        w_bc=((rows, 2, state), FULL),
        w_dt=((hc, rows), FULL),
        conv_x=((hc, taps, hw), FULL),
        conv_bc=((2, taps, state), FULL),
        dt_bias=((1, hc), FULL),
        a_log=((1, hc), FULL),
        skip=((1, hc), FULL),
        gate_gain=((hc, hw), FULL),
    )
    specs += [VMEM_SPEC] * (len(shapes) - len(specs))
    given = dict(vars(made), cot=cot)
    results = pl.pallas_call(
        partial(finish_kernel, dims, list(given), list(large), list(shapes)),
        out_shape=[jax.ShapeDtypeStruct(*shape) for shape in shapes.values()],
        in_specs=[VMEM_SPEC] * len(given),
        out_specs=specs,
        scratch_shapes=[pltpu.VMEM((T, D), FULL), pltpu.SemaphoreType.DMA((len(large) + 4,))],
        name="finish",
    )(*given.values())
    return SimpleNamespace(**dict(zip(shapes, results)))


def on_device(
    block_in, cotangent, norm_gain, w_x, w_z, w_bc, w_dt, conv_x, conv_bc, dt_bias, a_log, skip,
    gate_gain, w_out,
):
    length, width = block_in.shape
    hc, hw, taps = conv_x.shape
    state = conv_bc.shape[1]
    inner = hc * hw
    heads, tensors, count = (lax.axis_size(a) for a in ("head", "tensor", "fsdp"))
    size = heads * tensors
    quarter = 2 * state // size
    rows = w_x.shape[0]
    block = Block(count, rows)
    used = quarter + hc
    side_rows = used + -used % 16 if block.turned else used + -used % LANES
    assert hw & (hw - 1) == 0 and LANES % hw == 0
    turn = lambda a: a if block.turned else a.T
    arrays = dict(
        wx=turn(w_x.transpose(1, 2, 0).reshape(inner, rows)),
        w_bc=w_bc,
        w_dt=w_dt.T,
        x_in=block_in,
        norm_gain=norm_gain[None, :],
        cot=cotangent,
        wz=turn(w_z.transpose(1, 2, 0).reshape(inner, rows)),
        wo=turn(w_out.reshape(inner, rows)),
        conv_x=conv_x.transpose(0, 2, 1),
        conv_bc=conv_bc.transpose(0, 2, 1),
        dt_bias=dt_bias[None, :],
        a_log=a_log[None, :],
        skip=skip[None, :],
        gate_gain=gate_gain,
    )
    dims = dict(
        count=count, heads=heads, tensors=tensors, hw=hw, hc=hc, taps=taps, state=state,
        quarter=quarter, block=block, side_rows=side_rows,
    )
    got = finish(dims, fused(dims, arrays), cotangent)
    by_weight = lambda a: turn(a).reshape(hc, hw, rows)
    return (
        got.block_out,
        got.grad_in,
        got.norm_grad.reshape(width),
        by_weight(got.own_x).transpose(2, 0, 1),
        by_weight(got.own_z).transpose(2, 0, 1),
        got.w_bc,
        got.w_dt.T,
        got.conv_x.transpose(0, 2, 1),
        got.conv_bc.transpose(0, 2, 1),
        got.dt_bias.reshape(hc),
        got.a_log.reshape(hc),
        got.skip.reshape(hc),
        got.gate_gain,
        by_weight(got.own_o),
    )


def solution(mesh):
    return jax.shard_map(
        on_device,
        mesh=mesh,
        in_specs=(
            P("fsdp", None),
            P("fsdp", None),
            P(),
            P("fsdp", "head", "tensor"),
            P("fsdp", "head", "tensor"),
            P("fsdp", None, None),
            P("fsdp", "head"),
            P("head", "tensor", None),
            P(),
            P("head"),
            P("head"),
            P("head"),
            P("head", "tensor"),
            P("head", "tensor", "fsdp"),
        ),
        out_specs=(
            P("fsdp", None),
            P("fsdp", None),
            P(),
            P("fsdp", "head", "tensor"),
            P("fsdp", "head", "tensor"),
            P("fsdp", None, None),
            P("fsdp", "head"),
            P("head", "tensor", None),
            P(),
            P("head"),
            P("head"),
            P("head"),
            P("head", "tensor"),
            P("head", "tensor", "fsdp"),
        ),
        check_vma=False,
    )
```

```python
from functools import partial
from types import SimpleNamespace

import jax
import jax.numpy as jnp
from jax import lax
from jax.experimental import pallas as pl
from jax.experimental.pallas import tpu as pltpu
from jax.sharding import PartitionSpec as P

EPSILON = 1e-05
PRECISE = lax.Precision.HIGHEST
LANES = 128
SPAN = 128
ROWS = 32
PIECES = 4
LATE_Z = 2
LATE_OUT = 4
VMEM_LIMIT = 60 * 1024 * 1024
MESH = pl.DeviceIdType.MESH
VMEM_SPEC = pl.BlockSpec(memory_space=pltpu.VMEM)
LOW = jnp.bfloat16
FULL = jnp.float32


def ring_index(position, count):
    high = position // (count // 2)
    return (1 - high) * 2 * position + high * (2 * (count - 1 - position) + 1)


def ring_position(index, count):
    odd = index % 2
    return (1 - odd) * (index // 2) + odd * (count - 1 - index // 2)


def last_axes(a, b):
    return lax.dot_general(a, b, (((1,), (1,)), ((), ())), preferred_element_type=FULL)


def first_axes(a, b):
    return lax.dot_general(a, b, (((0,), (0,)), ((), ())), preferred_element_type=FULL)


def plain(a, b):
    return jnp.dot(a, b, preferred_element_type=FULL)


def high_low(value):
    high = value.astype(LOW)
    return high, (value - high.astype(FULL)).astype(LOW)


def sigmoid(value):
    return 1.0 / (1.0 + jnp.exp(-value))


def silu_slope(value, sigma):
    return sigma * (1.0 + value * (1.0 - sigma))


def softplus(value):
    return jnp.maximum(value, 0.0) + jnp.log1p(jnp.exp(-jnp.abs(value)))


def later(rows, amount):
    if amount == 0:
        return rows
    lane = lax.broadcasted_iota(jnp.int32, rows.shape, 1)
    return jnp.where(lane >= amount, pltpu.roll(rows, amount, 1), 0.0)


def sooner(rows, amount):
    if amount == 0:
        return rows
    length = rows.shape[1]
    lane = lax.broadcasted_iota(jnp.int32, rows.shape, 1)
    return jnp.where(lane < length - amount, pltpu.roll(rows, length - amount, 1), 0.0)


def own_lanes(hc, hw):
    shape = (hc, hc * hw)
    first = lax.broadcasted_iota(jnp.int32, shape, 0) * hw
    lane = lax.broadcasted_iota(jnp.int32, shape, 1)
    return (lane >= first) & (lane < first + hw)


def lane_places(hc, hw):
    shape = (hw, hc * hw)
    lane = lax.broadcasted_iota(jnp.int32, shape, 1)
    place = lax.broadcasted_iota(jnp.int32, shape, 0)
    return jnp.where(jnp.bitwise_and(lane, hw - 1) == place, 1.0, 0.0)


def group_peers(heads, tensors):
    head, tensor = lax.axis_index("head"), lax.axis_index("tensor")
    peers = []
    for offset in range(1, heads * tensors):
        peer_head = (head + offset // tensors) % heads
        peer_tensor = (tensor + offset % tensors) % tensors
        peers.append((peer_head, peer_tensor))
    return head * tensors + tensor, peers


class Block:

    def __init__(self, count, rows):
        self.count, self.rows = count, rows
        self.turned = rows % LANES == 0

    def shape(self, columns):
        return (columns, self.rows) if self.turned else (self.rows, columns)

    def halves(self, ref):
        unit = 16 if self.turned else LANES
        columns = ref.shape[0] if self.turned else ref.shape[1]
        first = (columns // unit + 1) // 2 * unit
        starts = [(0, first), (first, columns - first)] if first < columns else [(0, first)]
        return [self.slice(*start) for start in starts]

    def slice(self, start, amount):
        part = pl.ds(start, amount)
        return (part, slice(None)) if self.turned else (slice(None), part)

    def sizes(self, columns):
        shape = jax.ShapeDtypeStruct(self.shape(columns), LOW)
        return [
            (cut[0].size, self.rows) if self.turned else (self.rows, cut[1].size)
            for cut in self.halves(shape)
        ]

    def matrix(self, ref):
        if self.turned:
            return jnp.concatenate([ref[i] for i in range(self.count)], axis=1)
        return ref[...].reshape(self.count * self.rows, ref.shape[2])

    def project(self, a, matrix):
        return last_axes(a, matrix) if self.turned else plain(a, matrix)

    def back(self, a, matrix):
        return plain(a, matrix) if self.turned else last_axes(a, matrix)

    def store(self, ref, matrix):
        if self.turned:
            for i in range(self.count):
                ref[i] = matrix[:, i * self.rows : (i + 1) * self.rows].astype(ref.dtype)
        else:
            ref[...] = matrix.reshape(ref.shape).astype(ref.dtype)

    def gradient(self, act_ref, d_ref, out_ref):
        if self.turned:
            d = d_ref[...]
            for i in range(self.count):
                part = act_ref[:, i * self.rows : (i + 1) * self.rows]
                out_ref[i] = first_axes(d, part).astype(out_ref.dtype)
        else:
            self.store(out_ref, first_axes(act_ref[...], d_ref[...]))


def block_kernel(dims, given, names, sem_names, *args):
    ref = SimpleNamespace(**dict(zip(names, args)))
    pairs = args[len(names) :]
    sem = SimpleNamespace(
        **{name: (pairs[2 * i], pairs[2 * i + 1]) for i, name in enumerate(sem_names)}
    )
    count, heads, tensors, hw, taps, state, quarter = (
        dims[k] for k in ("count", "heads", "tensors", "hw", "taps", "state", "quarter")
    )
    loads = {
        name: pltpu.make_async_copy(
            getattr(ref, "raw_" + name), getattr(ref, name), args[-1].at[place]
        )
        for place, name in enumerate(given)
    }
    for copy in loads.values():
        copy.start()
    T, D = ref.x_in.shape
    hc = ref.skip.shape[1]
    I = hc * hw
    size = heads * tensors
    block = dims["block"]
    side_rows = dims["side_rows"]
    groups = I // LANES
    per = LANES // hw
    spans = T // SPAN
    head, tensor = lax.axis_index("head"), lax.axis_index("tensor")
    me = lax.axis_index("fsdp")
    group_me, peers = group_peers(heads, tensors)
    position = ring_position(me, count)
    right = ring_index((position + 1) % count, count)
    left = ring_index((position + count - 1) % count, count)
    others = [(me + offset) % count for offset in range(1, count)]
    head_peers = [(head + offset) % heads for offset in range(1, heads)]
    tensor_peers = [(tensor + offset) % tensors for offset in range(1, tensors)]
    started = []

    barrier = pltpu.get_barrier_semaphore()
    for h, t in peers:
        pl.semaphore_signal(barrier, inc=1, device_id={"head": h, "tensor": t}, device_id_type=MESH)
    for other in others:
        pl.semaphore_signal(barrier, inc=1, device_id={"fsdp": other}, device_id_type=MESH)
    pl.semaphore_wait(barrier, len(peers) + len(others))

    def send(source, target, sems, place, device):
        copy = pltpu.make_async_remote_copy(
            src_ref=source,
            dst_ref=target,
            send_sem=sems[0].at[place],
            recv_sem=sems[1].at[place],
            device_id=device,
            device_id_type=MESH,
        )
        copy.start()
        started.append(copy)
        return copy

    half_count = count // 2
    rights = [ring_index((position + count - i) % count, count) for i in range(half_count + 1)]
    lefts = [ring_index((position + i) % count, count) for i in range(half_count + 1)]

    def gather_part(shard, full, sems):
        cuts = block.halves(shard)
        copies = {}

        def step_at(step):
            if step == 0:
                full[me] = shard[...]
            for way, cut in enumerate(cuts):
                for turn, (target, owners) in enumerate(((right, rights), (left, lefts))):
                    if step > 0 and (step < half_count or way == turn):
                        copies[way, turn, step - 1].wait_recv()
                    if step < half_count - 1 or (step == half_count - 1 and way == turn):
                        place = full.at[(owners[step],) + cut]
                        source = shard.at[cut] if step == 0 else place
                        copies[way, turn, step] = send(
                            source, place, sems, (way, turn, step), {"fsdp": target}
                        )

        return step_at

    def scatter_part(grads, own, slots, sems):
        cuts = block.halves(own)
        copies = {}

        def step_at(step):
            for way, cut in enumerate(cuts):
                held = slots[way]
                if step == half_count:
                    total = grads[(me,) + cut].astype(FULL)
                    for turn in range(2):
                        copies[way, turn, step - 1].wait_recv()
                        total = total + held[turn, step - 1].astype(FULL)
                    own[cut] = total
                    continue
                for turn, (target, owners) in enumerate(((right, lefts), (left, rights))):
                    piece = (owners[half_count - step],) + cut
                    if step == 0 and way != turn:
                        continue
                    if step == 0 or (step == 1 and way != turn):
                        source = grads.at[piece]
                    else:
                        copies[way, turn, step - 1].wait_recv()
                        total = held[turn, step - 1].astype(FULL) + grads[piece].astype(FULL)
                        held[turn, step - 1] = total.astype(LOW)
                        source = held.at[turn, step - 1]
                    copies[way, turn, step] = send(
                        source, held.at[turn, step], sems, (way, turn, step), {"fsdp": target}
                    )

        return step_at

    def rounds(parts):
        keyed = [
            (late + step, place, step_at, step)
            for place, (late, step_at) in enumerate(parts)
            for step in range(half_count + 1)
        ]
        keyed.sort(key=lambda entry: entry[:2])
        return keyed

    queue = []

    def pump(amount):
        for _ in range(amount):
            if queue:
                key = queue[0][0]
                while queue and queue[0][0] == key:
                    _, _, step_at, step = queue.pop(0)
                    step_at(step)

    def pump_until(key):
        while queue and queue[0][0] <= key:
            pump(1)

    def row_loop(body, first=0, last=T):
        def run(i, carry):
            body(pl.multiple_of(first + i * ROWS, ROWS))
            return carry

        lax.fori_loop(0, (last - first) // ROWS, run, 0)

    queue += rounds(
        [
            (0, gather_part(ref.wx, ref.all_x, sem.gather_x)),
            (0, lambda step: side_part[0](step)),
            (LATE_Z, gather_part(ref.wz, ref.all_z, sem.gather_z)),
            (LATE_OUT, gather_part(ref.wo, ref.all_o, sem.gather_o)),
        ]
    )
    loads.pop("wx").wait()
    queue.pop(0)[2](0)
    loads.pop("w_bc").wait()
    loads.pop("w_dt").wait()
    maps = ref.w_bc[...].astype(FULL)
    maps = jnp.concatenate([maps[:, i, :] for i in range(2)], axis=1).T
    ref.maps[...] = maps
    mine_at = pl.ds(pl.multiple_of(group_me * quarter, quarter), quarter)
    side_list = [ref.maps[mine_at, :], ref.w_dt[...].astype(FULL)]
    if side_rows > quarter + hc:
        side_list.append(jnp.zeros((side_rows - quarter - hc, maps.shape[1]), FULL))
    side = jnp.concatenate(side_list, axis=0)
    ref.ws[...] = (side if block.turned else side.T).astype(LOW)
    side_part = [gather_part(ref.ws, ref.all_s, sem.gather_s)]
    pump(1)

    def norm_rows(r):
        at = pl.ds(r, ROWS)
        features = ref.x_in[at, :].astype(FULL)
        mean = jnp.mean(features * features, axis=1, keepdims=True)
        scale = lax.rsqrt(mean + EPSILON)
        ref.scale_in[at, :] = scale
        ref.normed[at, :] = (features * scale * ref.norm_gain[...]).astype(LOW)

    for copy in loads.values():
        copy.wait()
    row_loop(norm_rows)
    ref.x_pad[0:8, :] = jnp.zeros((8, I), FULL)
    ref.d_conv[T : T + 8, :] = jnp.zeros((8, I), FULL)
    ref.columns[...] = jnp.zeros((T, LANES), FULL)
    ref.sums[...] = jnp.zeros((8, I), FULL)

    ours = own_lanes(hc, hw)
    place_of = lane_places(hc, hw)
    equal = lax.broadcasted_iota(jnp.int32, (hc, hc), 0) == lax.broadcasted_iota(
        jnp.int32, (hc, hc), 1
    )

    def column(row_ref):
        return jnp.sum(jnp.where(equal, row_ref[...], 0.0), axis=1, keepdims=True)

    def spread(by_head):
        wide = jnp.dot(by_head, place_of, precision=PRECISE, preferred_element_type=FULL)
        return jnp.sum(jnp.where(ours, wide, 0.0), axis=0, keepdims=True)

    for k in range(taps):
        ref.kernel_x[k : k + 1, :] = spread(ref.conv_x[:, k, :])
    ref.gain[...] = spread(ref.gate_gain[...])
    ref.skip_wide[...] = jnp.sum(jnp.where(ours, column(ref.skip), 0.0), axis=0, keepdims=True)
    ref.kernel_all[...] = jnp.concatenate([ref.conv_bc[i].T for i in range(2)], axis=0)
    ref.kernel_bc[...] = ref.kernel_all[mine_at, :]
    expand = jnp.where(ours, 1.0, 0.0).astype(LOW)
    expand_two = jnp.concatenate([expand, expand], axis=0)

    def widen(rows):
        return first_axes(jnp.concatenate(high_low(rows), axis=0), expand_two)

    def narrow(wide):
        high, low = high_low(wide)
        return last_axes(expand, high) + last_axes(expand, low)

    pump_until(half_count)

    normed = ref.normed
    if block.turned:
        side = last_axes(block.matrix(ref.all_s), normed[...])
    else:
        side = plain(normed[...], block.matrix(ref.all_s)).T
    bc_raw = side[0:quarter]
    ref.bc_raw[...] = bc_raw
    kernel_bc = ref.kernel_bc
    bc_conv = sum(later(bc_raw, taps - 1 - k) * kernel_bc[:, k : k + 1] for k in range(taps))
    ref.bc_conv[...] = bc_conv
    ref.bc_mine[...] = (bc_conv * sigmoid(bc_conv)).astype(LOW)
    bc = ref.bc
    bc_copies = [
        send(ref.bc_mine, bc.at[mine_at, :], sem.bc, place, {"head": h, "tensor": t})
        for place, (h, t) in enumerate(peers)
    ]
    bc[mine_at, :] = ref.bc_mine[...]

    half = T // 2
    x_matrix = block.matrix(ref.all_x)
    for first in (0, half):
        ref.x_pad[8 + first : 8 + first + half, :] = block.project(
            normed[first : first + half, :], x_matrix
        )

    dt_in = side[quarter : quarter + hc] + column(ref.dt_bias)
    step = softplus(dt_in)
    rate = -jnp.exp(column(ref.a_log))
    logs = step * rate
    ref.dt_in[...] = dt_in
    ref.step[...] = step
    sooner_row = lax.broadcasted_iota(jnp.int32, (SPAN, SPAN), 0)
    later_lane = lax.broadcasted_iota(jnp.int32, (SPAN, SPAN), 1)
    upper = jnp.where(sooner_row <= later_lane, 1.0, 0.0)
    lower = jnp.where(sooner_row >= later_lane, 1.0, 0.0)
    causal = sooner_row >= later_lane
    cums, to_end = [], []
    for c in range(spans):
        part = jnp.dot(
            logs[:, c * SPAN : (c + 1) * SPAN], upper, precision=PRECISE, preferred_element_type=FULL
        )
        cums.append(part)
        to_end.append(part[:, SPAN - 1 : SPAN] - part)
    cums = jnp.concatenate(cums, axis=1)
    ref.cums[...] = cums
    ref.cum_columns[...] = cums.T
    ref.from_start[...] = widen(jnp.exp(cums))
    ref.to_end[...] = widen(jnp.exp(jnp.concatenate(to_end, axis=1)))
    ref.step_wide[...] = widen(step)

    kernel_x = ref.kernel_x

    def conv_rows(r):
        at = pl.ds(r, ROWS)
        near = ref.x_pad[pl.ds(r, ROWS + 8), :]
        conv = sum(
            kernel_x[k : k + 1, :] * near[9 - taps + k : 9 - taps + k + ROWS] for k in range(taps)
        )
        ref.conv[at, :] = conv
        act = (conv * sigmoid(conv)).astype(LOW)
        ref.act[at, :] = act
        v = act.astype(FULL) * ref.step_wide[at, :]
        ref.v[at, :] = v.astype(LOW)
        ref.v_end[at, :], ref.v_end_low[at, :] = high_low(v * ref.to_end[at, :])

    row_loop(conv_rows)
    pump(1)
    for copy in bc_copies:
        copy.wait_recv()

    head_lane = lax.broadcasted_iota(jnp.int32, (SPAN, LANES), 1)
    lanes_of = [(head_lane >= i * hw) & (head_lane < (i + 1) * hw) for i in range(per)]

    def maps_of(c):
        at = slice(c * SPAN, (c + 1) * SPAN)
        return bc[0:state, at], bc[state : 2 * state, at]

    def decay_of(c, h):
        at = slice(c * SPAN, (c + 1) * SPAN)
        gap = ref.cum_columns[at, h : h + 1] - ref.cums[h : h + 1, at]
        return jnp.exp(jnp.where(causal, gap, -1e30))

    y = ref.y
    for c in range(spans):
        at = slice(c * SPAN, (c + 1) * SPAN)
        b_map, c_map = maps_of(c)
        scores = first_axes(c_map, b_map)
        if c > 0:
            y[at, :] = (first_axes(c_map, ref.states[c]) + first_axes(c_map, ref.states_low[c])) * ref.from_start[at, :]
        for g in range(groups):
            lanes = slice(g * LANES, (g + 1) * LANES)
            v = ref.v[at, lanes]
            weights, values = [], []
            for i in range(per):
                weights.append((scores * decay_of(c, g * per + i)).astype(LOW))
                values.append(jnp.where(lanes_of[i], v, jnp.zeros_like(v)))
            part = plain(jnp.concatenate(weights, axis=1), jnp.concatenate(values, axis=0))
            y[at, lanes] = part if c == 0 else y[at, lanes] + part
        if c + 1 < spans:
            new = plain(b_map, ref.v_end[at, :]) + plain(b_map, ref.v_end_low[at, :])
            if c > 0:
                whole = ref.from_start[(c + 1) * SPAN - 1 : (c + 1) * SPAN, :]
                new = ref.running[...] * whole + new
            ref.running[...] = new
            ref.states[c + 1], ref.states_low[c + 1] = high_low(new)

    pump_until(LATE_Z + half_count)
    z_matrix = block.matrix(ref.all_z)
    for first in (0, half):
        ref.z[first : first + half, :] = block.project(normed[first : first + half, :], z_matrix)
    skip = ref.skip_wide
    gain = ref.gain
    columns = ref.columns

    def gate_rows(r):
        at = pl.ds(r, ROWS)
        z = ref.z[at, :]
        mixed = y[at, :] + skip[...] * ref.act[at, :].astype(FULL)
        gated = mixed * (z * sigmoid(z))
        ref.gated[at, :] = gated
        columns[at, 0:1] = jnp.sum(gated * gated, axis=1, keepdims=True)

    row_loop(gate_rows)

    def exchanged(lane, mine, everyone, sems):
        mine[...] = columns[...].T[lane : lane + 1]
        everyone[group_me] = mine[...]
        copies = [
            send(mine, everyone.at[group_me], sems, place, {"head": h, "tensor": t})
            for place, (h, t) in enumerate(peers)
        ]
        pump(1)
        for copy in copies:
            copy.wait_recv()
        total = everyone[0]
        for k in range(1, size):
            total = total + everyone[k]
        return total

    full_inner = I * size
    squares = exchanged(0, ref.square, ref.squares, sem.square)
    scale_row = lax.rsqrt(squares / full_inner + EPSILON)
    ref.scale_row[...] = scale_row
    ref.scales[...] = jnp.concatenate([scale_row, jnp.zeros((7, T), FULL)], axis=0).T

    def normed_out_rows(r):
        at = pl.ds(r, ROWS)
        hat = ref.gated[at, :] * ref.scales[at, 0:1]
        ref.normed_out[at, :] = (hat * gain[...]).astype(LOW)

    row_loop(normed_out_rows)
    block.gradient(ref.cot, ref.normed_out, ref.g_o)
    scatter_o = scatter_part(ref.g_o, ref.own_o, (ref.slot_o0, ref.slot_o1), sem.scatter_o)
    scatter_z = scatter_part(ref.g_z, ref.own_z, (ref.slot_z0, ref.slot_z1), sem.scatter_z)
    scatter_x = scatter_part(ref.g_x, ref.own_x, (ref.slot_x0, ref.slot_x1), sem.scatter_x)
    scatter_s = scatter_part(ref.g_s, ref.own_s, (ref.slot_s0, ref.slot_s1), sem.scatter_s)
    last_key = LATE_OUT + half_count

    def enqueue(parts, key):
        for place, step_at in enumerate(parts):
            queue.extend((key + step, place, step_at, step) for step in range(1, half_count + 1))
        queue.sort(key=lambda entry: entry[:2])

    scatter_o(0)
    enqueue([scatter_o], last_key - 1.5)
    pump_until(last_key)

    o_matrix = block.matrix(ref.all_o)
    for first in (0, half):
        ref.d_no[first : first + half, :] = block.project(
            ref.cot[first : first + half, :], o_matrix
        )

    def inner_rows(r):
        at = pl.ds(r, ROWS)
        columns[at, 1:2] = jnp.sum(
            ref.d_no[at, :] * gain[...] * ref.gated[at, :], axis=1, keepdims=True
        )

    row_loop(inner_rows)
    inner_sum = exchanged(1, ref.product, ref.products, sem.product)
    scale_row = ref.scale_row[...]
    third_row = scale_row * scale_row * scale_row * (inner_sum / full_inner)
    ref.thirds[...] = jnp.concatenate([third_row, jnp.zeros((7, T), FULL)], axis=0).T

    def gate_back_rows(r):
        at = pl.ds(r, ROWS)
        scale = ref.scales[at, 0:1]
        third = ref.thirds[at, 0:1]
        gated, d_no, z = ref.gated[at, :], ref.d_no[at, :], ref.z[at, :]
        act = ref.act[at, :].astype(FULL)
        hat = gated * scale
        d_gated = scale * (d_no * gain[...]) - gated * third
        sigma = sigmoid(z)
        d_mixed = d_gated * (z * sigma)
        mixed = y[at, :] + skip[...] * act
        ref.d_z[at, :] = (d_gated * mixed * silu_slope(z, sigma)).astype(LOW)
        ref.d_mixed[at, :] = d_mixed
        ref.dy[at, :] = d_mixed.astype(LOW)
        ref.dy_start[at, :], ref.dy_start_low[at, :] = high_low(d_mixed * ref.from_start[at, :])
        ref.sums[0:1, :] += jnp.sum(d_no * hat, axis=0, keepdims=True)
        ref.sums[1:2, :] += jnp.sum(d_mixed * act, axis=0, keepdims=True)

    row_loop(gate_back_rows)

    pump(1)
    block.gradient(normed, ref.d_z, ref.g_z)
    scatter_z(0)
    enqueue([scatter_z], last_key + 1.2)

    share = T // heads
    piece = share // PIECES

    class GroupSum:
        def __init__(self, source, result, finish, held, sems):
            self.source, self.result, self.finish = source, result, finish
            self.by_head, self.middle, self.by_tensor = held
            self.sems = sems
            self.from_head, self.from_tensor, self.back = {}, {}, {}

        def rows(self, h, j):
            return pl.ds(pl.multiple_of(h * share + j * piece, piece), piece)

        def start(self, j):
            self.from_head[j] = [
                send(
                    self.source.at[self.rows(peer, j), :], self.by_head.at[j, k], self.sems[0],
                    (j, k), {"head": peer},
                )
                for k, peer in enumerate(head_peers)
            ]

        def across(self, j):
            for copy in self.from_head[j]:
                copy.wait_recv()
            total = self.source[self.rows(head, j), :].astype(FULL)
            for k in range(heads - 1):
                total = total + self.by_head[j, k].astype(FULL)
            total = total.astype(LOW)
            self.middle[j] = total
            self.by_tensor[j, tensor] = total
            self.from_tensor[j] = [
                send(
                    self.middle.at[j], self.by_tensor.at[j, tensor], self.sems[1], (j, k),
                    {"tensor": peer},
                )
                for k, peer in enumerate(tensor_peers)
            ]

        def close(self, j):
            for copy in self.from_tensor[j]:
                copy.wait_recv()
            total = self.by_tensor[j, 0].astype(FULL)
            for k in range(1, tensors):
                total = total + self.by_tensor[j, k].astype(FULL)
            at = self.rows(head, j)
            self.result[at, :] = self.finish(at, total).astype(LOW)
            self.back[j] = [
                send(
                    self.result.at[at, :], self.result.at[at, :], self.sems[2], (j, k),
                    {"head": peer},
                )
                for k, peer in enumerate(head_peers)
            ]

        def end(self):
            for j in range(PIECES):
                for copy in self.back[j]:
                    copy.wait_recv()

    def finish_out(at, total):
        return total + ref.x_in[at, :].astype(FULL)

    norm_gain = ref.norm_gain

    def finish_in(at, total):
        features = ref.x_in[at, :].astype(FULL)
        scale = ref.scale_in[at, :]
        ref.norm_sum[0:1, :] += jnp.sum(total * (features * scale), axis=0, keepdims=True)
        inner = total * norm_gain[...]
        mean = jnp.mean(inner * features, axis=1, keepdims=True)
        return scale * inner - features * (scale * scale * scale * mean)

    out_sum = GroupSum(
        ref.partial_out, ref.block_out, finish_out, (ref.out_a, ref.out_m, ref.out_b),
        (sem.out_a, sem.out_b, sem.out_c),
    )
    in_sum = GroupSum(
        ref.partial_in, ref.low_in, finish_in, (ref.in_a, ref.in_m, ref.in_b),
        (sem.in_a, sem.in_b, sem.in_c),
    )
    for first in (0, half):
        ref.partial_out[first : first + half, :] = block.back(
            ref.normed_out[first : first + half, :], o_matrix
        ).astype(LOW)
    for j in range(PIECES):
        out_sum.start(j)

    d_bc = ref.d_bc
    d_row = []
    for c in reversed(range(spans)):
        at = slice(c * SPAN, (c + 1) * SPAN)
        b_map, c_map = maps_of(c)
        scores = first_axes(c_map, b_map)
        d_scores = jnp.zeros((SPAN, SPAN), FULL)
        last = c + 1 == spans
        if not last:
            low_d_state, lower_d_state = high_low(ref.d_state[...])
            ref.u[at, :] = (first_axes(b_map, low_d_state) + first_axes(b_map, lower_d_state)) * ref.to_end[at, :]
        for g in range(groups):
            lanes = slice(g * LANES, (g + 1) * LANES)
            v = ref.v[at, lanes]
            dy = ref.dy[at, lanes]
            dy_turned = dy.astype(FULL).T.astype(LOW)
            lane_row = lax.broadcasted_iota(jnp.int32, (LANES, SPAN), 0)
            weights, values = [], []
            for i in range(per):
                decay = decay_of(c, g * per + i)
                weights.append((scores * decay).astype(LOW))
                mine = (lane_row >= i * hw) & (lane_row < (i + 1) * hw)
                values.append(jnp.where(mine, dy_turned, jnp.zeros_like(dy_turned)))
                own_dy = jnp.where(lanes_of[i], dy, jnp.zeros_like(dy))
                d_scores = d_scores + last_axes(own_dy, v) * decay
            part = plain(jnp.concatenate(values, axis=1), jnp.concatenate(weights, axis=0)).T
            ref.u[at, lanes] = part if last else ref.u[at, lanes] + part
        low_d = d_scores.astype(LOW)
        d_b = plain(c_map, low_d)
        d_c = last_axes(b_map, low_d)
        if not last:
            d_b = d_b + last_axes(low_d_state, ref.v_end[at, :])
        if c > 0:
            d_c = d_c + last_axes(ref.states[c], ref.dy_start[at, :])
        d_bc[0:state, at] = d_b.astype(LOW)
        d_bc[state : 2 * state, at] = d_c.astype(LOW)

        u = ref.u[at, :]
        balance = narrow(
            ref.dy[at, :].astype(FULL) * y[at, :] - ref.v[at, :].astype(FULL) * u
        )
        d_logs = jnp.dot(balance, lower, precision=PRECISE, preferred_element_type=FULL)
        if not last:
            passed = jnp.sum(
                (ref.states[c + 1].astype(FULL) + ref.states_low[c + 1].astype(FULL)) * ref.d_state[...], axis=0, keepdims=True
            )
            passed = jnp.sum(jnp.where(ours, passed, 0.0), axis=1, keepdims=True)
            d_logs = d_logs + passed
        d_step = narrow(ref.act[at, :].astype(FULL) * u)
        d_row.append((d_logs, d_step))
        if c > 0:
            new = plain(c_map, ref.dy_start[at, :]) + plain(c_map, ref.dy_start_low[at, :])
            if not last:
                whole = ref.from_start[(c + 1) * SPAN - 1 : (c + 1) * SPAN, :]
                new = ref.d_state[...] * whole + new
            ref.d_state[...] = new
        if c == spans - 1:
            for j in range(PIECES):
                out_sum.across(j)
        pump(1)
    d_logs = jnp.concatenate([pair[0] for pair in reversed(d_row)], axis=1)
    d_step = jnp.concatenate([pair[1] for pair in reversed(d_row)], axis=1)
    step = ref.step[...]
    d_dt = (d_step + d_logs * rate) * sigmoid(ref.dt_in[...])
    g_a_log = jnp.sum(d_logs * step, axis=1, keepdims=True) * rate
    g_skip = jnp.sum(jnp.where(ours, ref.sums[1:2, :], 0.0), axis=1, keepdims=True)
    ref.d_dt[...] = d_dt

    small_copies = []
    for place, (h, t) in enumerate(peers):
        theirs = pl.ds(pl.multiple_of((h * tensors + t) * quarter, quarter), quarter)
        small_copies.append(
            send(
                d_bc.at[theirs, :], ref.held_bc.at[place], sem.share, place,
                {"head": h, "tensor": t},
            )
        )
    ref.held_dt[tensor] = ref.d_dt[...]
    for place, t in enumerate(tensor_peers):
        small_copies.append(
            send(ref.d_dt, ref.held_dt.at[tensor], sem.steps, place, {"tensor": t})
        )

    def slope_rows(r):
        at = pl.ds(r, ROWS)
        conv = ref.conv[at, :]
        d_xs = ref.step_wide[at, :] * ref.u[at, :] + skip[...] * ref.d_mixed[at, :]
        ref.d_conv[at, :] = d_xs * silu_slope(conv, sigmoid(conv))

    def unconv_rows(r):
        at = pl.ds(r, ROWS)
        near = ref.d_conv[pl.ds(r, ROWS + 8), :]
        raw = ref.x_pad[pl.ds(r, ROWS + 8), :]
        ref.d_x[at, :] = sum(
            kernel_x[k : k + 1, :] * near[taps - 1 - k : taps - 1 - k + ROWS] for k in range(taps)
        ).astype(LOW)
        for k in range(taps):
            ref.small_mine[k : k + 1, :] += jnp.sum(
                raw[9 - taps + k : 9 - taps + k + ROWS] * near[:ROWS], axis=0, keepdims=True
            )

    ref.small_mine[...] = jnp.zeros((8, I), FULL)
    row_loop(slope_rows)
    row_loop(unconv_rows)
    ref.small_mine[taps : taps + 1, :] = ref.sums[0:1, :]

    def to_others(source, everyone, sems):
        everyone[me] = source[...]
        return [
            send(source, everyone.at[me], sems, k, {"fsdp": other}) for k, other in enumerate(others)
        ]

    def summed(copies, everyone):
        for copy in copies:
            copy.wait_recv()
        value = everyone[0]
        for k in range(1, count):
            value = value + everyone[k]
        return value

    block.gradient(normed, ref.d_x, ref.g_x)
    scatter_x(0)
    pump(1)
    small_all = to_others(ref.small_mine, ref.all_small, sem.small)

    for copy in small_copies:
        copy.wait_recv()
    total_bc = d_bc[mine_at, :].astype(FULL)
    for place in range(size - 1):
        total_bc = total_bc + ref.held_bc[place].astype(FULL)
    total_dt = ref.held_dt[0]
    for t in range(1, tensors):
        total_dt = total_dt + ref.held_dt[t]
    conv = ref.bc_conv[...]
    d_conv = total_bc * silu_slope(conv, sigmoid(conv))
    d_bc_raw = sum(sooner(d_conv, taps - 1 - k) * kernel_bc[:, k : k + 1] for k in range(taps))
    raw = ref.bc_raw[...]
    g_bc = [
        jnp.sum(later(raw, taps - 1 - k) * d_conv, axis=1, keepdims=True) for k in range(taps)
    ]
    blank = jnp.zeros((hc, 1), FULL)
    below = [jnp.sum(total_dt, axis=1, keepdims=True), g_a_log, g_skip] + [blank] * taps
    ref.turn[...] = jnp.zeros((LANES, LANES), FULL)
    for k in range(taps):
        ref.turn[0:quarter, k : k + 1] = g_bc[k]
        ref.turn[quarter : quarter + hc, k : k + 1] = below[k]
    ref.tiny_mine[...] = ref.turn[...].T[0:8]
    tiny_all = to_others(ref.tiny_mine, ref.all_tiny, sem.tiny)
    side_list = [d_bc_raw, total_dt]
    if side_rows > quarter + hc:
        side_list.append(jnp.zeros((side_rows - quarter - hc, T), FULL))
    d_side = jnp.concatenate(side_list, axis=0).astype(LOW)
    s_matrix = block.matrix(ref.all_s)
    if block.turned:
        block.store(ref.g_s, plain(d_side, normed[...]))
    else:
        block.store(ref.g_s, plain(d_side, normed[...]).T)
        s_matrix = s_matrix.astype(FULL).T.astype(LOW)
    scatter_s(0)
    enqueue([scatter_x, scatter_s], last_key + 4.6)
    row = lax.broadcasted_iota(jnp.int32, (side_rows, T), 0)
    once = jnp.where(tensor == 0, quarter + hc, quarter)
    d_side = jnp.where(row < once, d_side.astype(FULL), 0.0).astype(LOW)
    x_matrix = block.matrix(ref.all_x)
    z_matrix = block.matrix(ref.all_z)
    ref.norm_sum[...] = jnp.zeros((1, D), FULL)
    for j in range(PIECES):
        out_sum.close(j)

    def back_piece(h, j):
        at = in_sum.rows(h, j)
        ref.partial_in[at, :] = (
            block.back(ref.d_x[at, :], x_matrix) + block.back(ref.d_z[at, :], z_matrix)
            + ref.side_in[at, :]
        ).astype(LOW)

    ref.side_in[...] = first_axes(d_side, s_matrix)
    for j in range(PIECES):
        for h in head_peers:
            back_piece(h, j)
        in_sum.start(j)
    pump(1)
    for j in range(PIECES):
        back_piece(head, j)
        in_sum.across(j)
    for j in range(PIECES):
        pump(1)
        in_sum.close(j)
    ref.norm_mine[...] = ref.norm_sum[...]
    ref.norm_heads[head] = ref.norm_sum[...]
    norm_copies = [
        send(ref.norm_mine, ref.norm_heads.at[head], sem.heads, k, {"head": peer})
        for k, peer in enumerate(head_peers)
    ]
    ref.small[...] = summed(small_all, ref.all_small)
    tiny = summed(tiny_all, ref.all_tiny)
    ref.tiny_sum[...] = tiny
    ref.tiny[group_me] = tiny
    tiny_copies = [
        send(ref.tiny_sum, ref.tiny.at[group_me], sem.gtiny, k, {"head": h, "tensor": t})
        for k, (h, t) in enumerate(peers)
    ]
    for copy in norm_copies:
        copy.wait_recv()
    total = ref.norm_heads[0]
    for k in range(1, heads):
        total = total + ref.norm_heads[k]
    ref.norm_total[...] = total
    norm_all = to_others(ref.norm_total, ref.all_norm, sem.norm)
    pump(4 * count)
    own_bc = ref.own_s[block.slice(0, quarter)]
    ref.own_bc[...] = own_bc if block.turned else ref.own_s[...].T[0:quarter]
    ref.bc_grad[group_me] = ref.own_bc[...]
    own_copies = [
        send(ref.own_bc, ref.bc_grad.at[group_me], sem.gbc, k, {"head": h, "tensor": t})
        for k, (h, t) in enumerate(peers)
    ]
    in_sum.end()
    out_sum.end()
    ref.norm_grad[...] = summed(norm_all, ref.all_norm)
    for copy in tiny_copies + own_copies:
        copy.wait_recv()
    for copy in started:
        copy.wait_send()


def fused(dims, arrays):
    count, heads, tensors = dims["count"], dims["heads"], dims["tensors"]
    taps, state, quarter, side_rows = (dims[k] for k in ("taps", "state", "quarter", "side_rows"))
    block, hw = dims["block"], dims["hw"]
    T, D = arrays["x_in"].shape
    hc = arrays["skip"].shape[1]
    I = hc * hw
    rows, size = D // count, heads * tensors
    spans = T // SPAN
    share = T // heads
    piece = share // PIECES
    wide, low_wide = ((T, I), FULL), ((T, I), LOW)
    shared = lambda columns: ((count,) + block.shape(columns), LOW)
    outs = dict(
        block_out=((T, D), LOW),
        low_in=((T, D), LOW),
        norm_grad=((1, D), FULL),
        own_x=(block.shape(I), FULL),
        own_s=(block.shape(side_rows), FULL),
        own_z=(block.shape(I), FULL),
        own_o=(block.shape(I), FULL),
        small=((8, I), FULL),
        tiny=((size, 8, LANES), FULL),
        bc_grad=((size, quarter, rows), FULL),
    )
    scratch = dict(
        all_x=shared(I),
        g_x=shared(I),
        all_s=shared(side_rows),
        g_s=shared(side_rows),
        all_z=shared(I),
        g_z=shared(I),
        all_o=shared(I),
        g_o=shared(I),
        conv=wide,
        y=wide,
        z=wide,
        gated=wide,
        d_no=wide,
        d_mixed=wide,
        u=wide,
        from_start=wide,
        to_end=wide,
        step_wide=wide,
        act=low_wide,
        v=low_wide,
        v_end=low_wide,
        v_end_low=low_wide,
        normed_out=low_wide,
        d_z=low_wide,
        dy=low_wide,
        dy_start=low_wide,
        dy_start_low=low_wide,
        d_x=low_wide,
        maps=((2 * state, rows), FULL),
        ws=(block.shape(side_rows), LOW),
        kernel_x=((8, I), FULL),
        kernel_all=((2 * state, taps), FULL),
        kernel_bc=((quarter, taps), FULL),
        skip_wide=((1, I), FULL),
        gain=((1, I), FULL),
        x_pad=((T + 8, I), FULL),
        d_conv=((T + 8, I), FULL),
        normed=((T, D), LOW),
        scale_in=((T, 1), FULL),
        columns=((T, LANES), FULL),
        sums=((8, I), FULL),
        bc_raw=((quarter, T), FULL),
        bc_conv=((quarter, T), FULL),
        bc_mine=((quarter, T), LOW),
        bc=((2 * state, T), LOW),
        dt_in=((hc, T), FULL),
        step=((hc, T), FULL),
        cums=((hc, T), FULL),
        cum_columns=((T, hc), FULL),
        running=((state, I), FULL),
        d_state=((state, I), FULL),
        states=((spans, state, I), LOW),
        states_low=((spans, state, I), LOW),
        square=((1, T), FULL),
        squares=((size, 1, T), FULL),
        product=((1, T), FULL),
        products=((size, 1, T), FULL),
        scale_row=((1, T), FULL),
        thirds=((T, 8), FULL),
        scales=((T, 8), FULL),
        partial_out=((T, D), LOW),
        partial_in=((T, D), LOW),
        side_in=((T, D), FULL),
        d_bc=((2 * state, T), LOW),
        held_bc=((size - 1, quarter, T), LOW),
        d_dt=((hc, T), FULL),
        held_dt=((tensors, hc, T), FULL),
        small_mine=((8, I), FULL),
        all_small=((count, 8, I), FULL),
        turn=((LANES, LANES), FULL),
        tiny_mine=((8, LANES), FULL),
        tiny_sum=((8, LANES), FULL),
        all_tiny=((count, 8, LANES), FULL),
        norm_sum=((1, D), FULL),
        norm_mine=((1, D), FULL),
        norm_total=((1, D), FULL),
        norm_heads=((heads, 1, D), FULL),
        all_norm=((count, 1, D), FULL),
        own_bc=((quarter, rows), FULL),
        out_a=((PIECES, heads - 1, piece, D), LOW),
        out_m=((PIECES, piece, D), LOW),
        out_b=((PIECES, tensors, piece, D), LOW),
        in_a=((PIECES, heads - 1, piece, D), LOW),
        in_m=((PIECES, piece, D), LOW),
        in_b=((PIECES, tensors, piece, D), LOW),
    )
    by_way = lambda columns: [((2, count // 2) + size, LOW) for size in block.sizes(columns)] * 2
    for some in (
        dict(zip(("slot_x0", "slot_x1"), by_way(I))),
        dict(zip(("slot_s0", "slot_s1"), by_way(side_rows))),
        dict(zip(("slot_z0", "slot_z1"), by_way(I))),
        dict(zip(("slot_o0", "slot_o1"), by_way(I))),
    ):
        scratch |= some
    ring = (2, 2, count // 2)
    sems = dict(
        bc=(size - 1,),
        square=(size - 1,),
        product=(size - 1,),
        share=(size - 1,),
        steps=(tensors - 1,),
        small=(count - 1,),
        tiny=(count - 1,),
        norm=(count - 1,),
        heads=(heads - 1,),
        gtiny=(size - 1,),
        gbc=(size - 1,),
        gather_x=ring, gather_s=ring, gather_z=ring, gather_o=ring,
        scatter_x=ring, scatter_s=ring, scatter_z=ring, scatter_o=ring,
        out_a=(PIECES, heads - 1),
        out_b=(PIECES, tensors - 1),
        out_c=(PIECES, heads - 1),
        in_a=(PIECES, heads - 1),
        in_b=(PIECES, tensors - 1),
        in_c=(PIECES, heads - 1),
    )
    scratch |= {name: (array.shape, array.dtype) for name, array in arrays.items()}
    names = ["raw_" + name for name in arrays] + list(outs) + list(scratch)
    scratch_shapes = [pltpu.VMEM(*shape) for shape in scratch.values()]
    for shape in sems.values():
        scratch_shapes += [pltpu.SemaphoreType.DMA(shape)] * 2
    scratch_shapes.append(pltpu.SemaphoreType.DMA((len(arrays),)))
    results = pl.pallas_call(
        partial(block_kernel, dims, list(arrays), names, list(sems)),
        out_shape=[jax.ShapeDtypeStruct(*shape) for shape in outs.values()],
        in_specs=[pl.BlockSpec(memory_space=pltpu.HBM)] * len(arrays),
        out_specs=[VMEM_SPEC] * len(outs),
        scratch_shapes=scratch_shapes,
        compiler_params=pltpu.CompilerParams(
            collective_id=0, has_side_effects=True, vmem_limit_bytes=VMEM_LIMIT
        ),
        name="block",
    )(*arrays.values())
    return SimpleNamespace(**dict(zip(outs, results)))


def finish_kernel(dims, names, passed, results, *args):
    heads, tensors, hw, hc, taps, state, quarter = (
        dims[k] for k in ("heads", "tensors", "hw", "hc", "taps", "state", "quarter")
    )
    given = SimpleNamespace(**dict(zip(names, args)))
    rest = args[len(names) :]
    out = SimpleNamespace(**dict(zip(results, rest)))
    staged, sems = rest[len(results) :]
    T = given.cot.shape[0]
    copies = [
        pltpu.make_async_copy(getattr(given, name), getattr(out, name), sems.at[i])
        for i, name in enumerate(passed)
    ]
    for copy in copies:
        copy.start()
    pieces = 4
    part = T // pieces
    for j in range(pieces):
        at = slice(j * part, (j + 1) * part)

        def grad_rows(i, carry):
            rows = pl.ds(pl.multiple_of(j * part + i * ROWS, ROWS), ROWS)
            staged[rows, :] = given.low_in[rows, :].astype(FULL) + given.cot[
                rows, :
            ].astype(FULL)
            return carry

        lax.fori_loop(0, part // ROWS, grad_rows, 0)
        copy = pltpu.make_async_copy(
            staged.at[at, :], out.grad_in.at[at, :], sems.at[len(passed) + j]
        )
        copy.start()
        copies.append(copy)
    head, tensor = lax.axis_index("head"), lax.axis_index("tensor")
    ours = own_lanes(hc, hw)
    place_of = lane_places(hc, hw)

    def gathered(row):
        return lax.dot_general(
            jnp.where(ours, row, 0.0), place_of, (((1,), (1,)), ((), ())), precision=PRECISE,
            preferred_element_type=FULL,
        )

    out.norm_grad[...] = given.norm_grad[0:1, :]
    maps = jnp.concatenate([given.bc_grad[i] for i in range(heads * tensors)], axis=0).T
    for i in range(2):
        out.w_bc[:, i, :] = maps[:, i * state : (i + 1) * state]
    turned = dims["block"].turned
    side = given.own_s[...] if turned else given.own_s[...].T
    out.w_dt[...] = side[quarter : quarter + hc]
    for k in range(taps):
        out.conv_x[:, k, :] = gathered(given.small[k : k + 1, :])
    out.gate_gain[...] = gathered(given.small[taps : taps + 1, :])
    tiny = given.tiny
    each = state // quarter
    for i in range(2):
        out.conv_bc[i] = jnp.concatenate(
            [tiny[i * each + j][0:taps, 0:quarter] for j in range(each)], axis=1
        )
    lanes = slice(quarter, quarter + hc)
    out.dt_bias[...] = tiny[head * tensors + tensor][0:1, lanes]
    by_head = tiny[head * tensors]
    for t in range(1, tensors):
        by_head = by_head + tiny[head * tensors + t]
    out.a_log[...] = by_head[1:2, lanes]
    out.skip[...] = by_head[2:3, lanes]
    for copy in copies:
        copy.wait()


def finish(dims, made, cot):
    T, D = cot.shape
    hc, hw, taps, state = (dims[k] for k in ("hc", "hw", "taps", "state"))
    rows = made.bc_grad.shape[2]
    any_spec = pl.BlockSpec(memory_space=pl.ANY)
    large = dict(
        block_out=made.block_out, own_x=made.own_x, own_z=made.own_z, own_o=made.own_o
    )
    shapes = {name: (array.shape, array.dtype) for name, array in large.items()}
    shapes |= dict(grad_in=((T, D), FULL))
    specs = [any_spec] * len(shapes)
    shapes |= dict(
        norm_grad=((1, D), FULL),
        w_bc=((rows, 2, state), FULL),
        w_dt=((hc, rows), FULL),
        conv_x=((hc, taps, hw), FULL),
        conv_bc=((2, taps, state), FULL),
        dt_bias=((1, hc), FULL),
        a_log=((1, hc), FULL),
        skip=((1, hc), FULL),
        gate_gain=((hc, hw), FULL),
    )
    specs += [VMEM_SPEC] * (len(shapes) - len(specs))
    given = dict(vars(made), cot=cot)
    results = pl.pallas_call(
        partial(finish_kernel, dims, list(given), list(large), list(shapes)),
        out_shape=[jax.ShapeDtypeStruct(*shape) for shape in shapes.values()],
        in_specs=[VMEM_SPEC] * len(given),
        out_specs=specs,
        scratch_shapes=[pltpu.VMEM((T, D), FULL), pltpu.SemaphoreType.DMA((len(large) + 4,))],
        name="finish",
    )(*given.values())
    return SimpleNamespace(**dict(zip(shapes, results)))


def on_device(
    block_in, cotangent, norm_gain, w_x, w_z, w_bc, w_dt, conv_x, conv_bc, dt_bias, a_log, skip,
    gate_gain, w_out,
):
    length, width = block_in.shape
    hc, hw, taps = conv_x.shape
    state = conv_bc.shape[1]
    inner = hc * hw
    heads, tensors, count = (lax.axis_size(a) for a in ("head", "tensor", "fsdp"))
    size = heads * tensors
    quarter = 2 * state // size
    rows = w_x.shape[0]
    block = Block(count, rows)
    used = quarter + hc
    side_rows = used + -used % 16 if block.turned else used + -used % LANES
    assert hw & (hw - 1) == 0 and LANES % hw == 0
    turn = lambda a: a if block.turned else a.T
    arrays = dict(
        wx=turn(w_x.transpose(1, 2, 0).reshape(inner, rows)),
        w_bc=w_bc,
        w_dt=w_dt.T,
        x_in=block_in,
        norm_gain=norm_gain[None, :],
        cot=cotangent,
        wz=turn(w_z.transpose(1, 2, 0).reshape(inner, rows)),
        wo=turn(w_out.reshape(inner, rows)),
        conv_x=conv_x.transpose(0, 2, 1),
        conv_bc=conv_bc.transpose(0, 2, 1),
        dt_bias=dt_bias[None, :],
        a_log=a_log[None, :],
        skip=skip[None, :],
        gate_gain=gate_gain,
    )
    dims = dict(
        count=count, heads=heads, tensors=tensors, hw=hw, hc=hc, taps=taps, state=state,
        quarter=quarter, block=block, side_rows=side_rows,
    )
    got = finish(dims, fused(dims, arrays), cotangent)
    by_weight = lambda a: turn(a).reshape(hc, hw, rows)
    return (
        got.block_out,
        got.grad_in,
        got.norm_grad.reshape(width),
        by_weight(got.own_x).transpose(2, 0, 1),
        by_weight(got.own_z).transpose(2, 0, 1),
        got.w_bc,
        got.w_dt.T,
        got.conv_x.transpose(0, 2, 1),
        got.conv_bc.transpose(0, 2, 1),
        got.dt_bias.reshape(hc),
        got.a_log.reshape(hc),
        got.skip.reshape(hc),
        got.gate_gain,
        by_weight(got.own_o),
    )


def solution(mesh):
    return jax.shard_map(
        on_device,
        mesh=mesh,
        in_specs=(
            P("fsdp", None),
            P("fsdp", None),
            P(),
            P("fsdp", "head", "tensor"),
            P("fsdp", "head", "tensor"),
            P("fsdp", None, None),
            P("fsdp", "head"),
            P("head", "tensor", None),
            P(),
            P("head"),
            P("head"),
            P("head"),
            P("head", "tensor"),
            P("head", "tensor", "fsdp"),
        ),
        out_specs=(
            P("fsdp", None),
            P("fsdp", None),
            P(),
            P("fsdp", "head", "tensor"),
            P("fsdp", "head", "tensor"),
            P("fsdp", None, None),
            P("fsdp", "head"),
            P("head", "tensor", None),
            P(),
            P("head"),
            P("head"),
            P("head"),
            P("head", "tensor"),
            P("head", "tensor", "fsdp"),
        ),
        check_vma=False,
    )
```
